128 devices in a mesh: gx: 8 (over y, z_lo), gy: 16 (over x, z_hi, core).
Axes of the slice: x: 4, y: 4, z: 4 (z_hi: 2, z_lo: 2; z = z_hi * 2 + z_lo), core: 2. Of those that a mesh axis runs over, the one named last changes fastest.
Arguments:
- selectors: float32 [3, 8, 8, 16, 65536], P(None, None, 'gx', 'gy'), may hold values from 0 to 2047, as said below
- proofs: float32 [3, 8, 8, 16, 65536], P(None, None, 'gx', 'gy'), may hold values from 0 to 2047, as said below
- challenges: int32 [4], replicated, may hold values from 0 to 2147483646
Outputs:
- round_values: float32 [3, 4, 3], replicated
- folded_selectors: float32 [3, 8, 8, 16, 4096], P(None, None, 'gx', 'gy')
- folded_proofs: float32 [3, 8, 8, 16, 4096], P(None, None, 'gx', 'gy')
The draws below stay inside these ranges and needn't reach their ends.
Inputs may be any that keep to these rules, and one draw needn't show every extreme that they name: `selectors`: limbs of field elements, as in the first step. `proofs`: limbs of field elements, as in the first step. `challenges`: field elements.
All inputs are finite; a program needn't handle non-finite values.
Results may differ from the reference program's by a relative error of at most 0.0003.
Values sent between devices are 32-bit elements; how exact they have to be, the bound alone decides.
A program may use at most 128 MiB of HBM per device.

```python
import jax
import jax.numpy as jnp
from jax import lax

PAIRS = 8
ROUNDS = 4
ROWS = 65536
XSPLIT = 8
YSPLIT = 16


def table_limbs(key):
    values = jax.random.randint(key, (PAIRS, XSPLIT, YSPLIT, ROWS), 0, 2147483647, dtype=jnp.int32)
    return jnp.stack([values & 2047, values >> 11 & 2047, values >> 22]).astype(jnp.float32)


def draw_selectors(key, part):
    return table_limbs(jax.random.fold_in(key, 11))


def draw_proofs(key, part):
    return table_limbs(jax.random.fold_in(key, 23))


def set_ends(values, key, low, top_value):
    longest = values.shape.index(max(values.shape))
    spots = []
    for shift in (0, 1):
        where = [jax.random.randint(jax.random.fold_in(key, axis), (), 0, length) for axis, length in enumerate(values.shape)]
        where[longest] = (where[longest] + shift) % values.shape[longest]
        spots.append(tuple(where))
    return values.at[spots[0]].set(low).at[spots[1]].set(top_value)


def setup_inputs(seed: int = 0) -> dict:
    key_list = jax.random.split(jax.random.key(seed), 4)
    selectors = draw_selectors(jax.random.fold_in(key_list[3], 71), 0)
    proofs = draw_proofs(jax.random.fold_in(key_list[3], 71), 0)
    challenges = set_ends(jax.random.randint(key_list[2], (ROUNDS,), 0, 2147483647), jax.random.fold_in(key_list[2], 1), 0, 2147483646).astype(jnp.int32)
    return {"selectors": selectors, "proofs": proofs, "challenges": challenges}


def settle(lowest, middle, highest):
    for repeat in range(3):
        carried = jnp.floor(lowest / 2048.0)
        lowest = lowest - carried * 2048.0
        middle = middle + carried
        carried = jnp.floor(middle / 2048.0)
        middle = middle - carried * 2048.0
        highest = highest + carried
        carried = jnp.floor(highest / 512.0)
        highest = highest - carried * 512.0
        lowest = lowest + carried
    at_modulus = (lowest == 2047.0) & (middle == 2047.0) & (highest == 511.0)
    nothing = jnp.zeros_like(lowest)
    return jnp.stack([jnp.where(at_modulus, nothing, lowest), jnp.where(at_modulus, nothing, middle), jnp.where(at_modulus, nothing, highest)])


def field_add(augend, addend):
    return settle(augend[0] + addend[0], augend[1] + addend[1], augend[2] + addend[2])


def field_sub(minuend, subtrahend):
    return settle(minuend[0] + 2047.0 - subtrahend[0], minuend[1] + 2047.0 - subtrahend[1], minuend[2] + 511.0 - subtrahend[2])


def field_mul(factor, multiplier):
    degree_zero = factor[0] * multiplier[0]
    degree_one = factor[0] * multiplier[1] + factor[1] * multiplier[0]
    degree_two = factor[0] * multiplier[2] + factor[1] * multiplier[1] + factor[2] * multiplier[0]
    degree_three = factor[1] * multiplier[2] + factor[2] * multiplier[1]
    degree_four = factor[2] * multiplier[2]
    carried = jnp.floor(degree_zero / 2048.0)
    degree_zero = degree_zero - carried * 2048.0
    degree_one = degree_one + carried
    carried = jnp.floor(degree_one / 2048.0)
    degree_one = degree_one - carried * 2048.0
    degree_two = degree_two + carried
    carried = jnp.floor(degree_two / 2048.0)
    degree_two = degree_two - carried * 2048.0
    degree_three = degree_three + carried
    carried = jnp.floor(degree_three / 2048.0)
    degree_three = degree_three - carried * 2048.0
    degree_four = degree_four + carried
    return settle(degree_zero + 4.0 * degree_three, degree_one + 4.0 * degree_four, degree_two)


def field_sum(values):
    values = values.reshape(3, -1)
    length = values.shape[1]
    while length > 1:
        stride = min(length, 2048)
        summed = values.reshape(3, length // stride, stride).sum(axis=2)
        values = settle(summed[0], summed[1], summed[2])
        length = length // stride
    return values.reshape(3)


def round_points(select_low, select_high, proof_low, proof_high):
    at_zero = field_sum(field_mul(select_low, proof_low))
    at_one = field_sum(field_mul(select_high, proof_high))
    select_two = field_sub(field_add(select_high, select_high), select_low)
    proof_two = field_sub(field_add(proof_high, proof_high), proof_low)
    at_two = field_sum(field_mul(select_two, proof_two))
    return jnp.stack([at_zero, at_one, at_two], axis=1)


def fold_tables(low_table, high_table, scalar):
    scalar = scalar.reshape((3,) + (1,) * (low_table.ndim - 1))
    return field_add(low_table, field_mul(field_sub(high_table, low_table), scalar))


def challenge_limbs(challenges, position):
    element = challenges[position]
    return jnp.stack([element & 2047, (element >> 11) & 2047, element >> 22]).astype(jnp.float32)


def split_top(values, position):
    shaped = values.shape
    reshaped = values.reshape(shaped[:position] + (2, shaped[position] // 2) + shaped[position + 1:])
    return lax.index_in_dim(reshaped, 0, position, keepdims=False), lax.index_in_dim(reshaped, 1, position, keepdims=False)


def reference(selectors, proofs, challenges):
    row_count = selectors.shape[-1]
    block_rows = min(row_count, 512)
    block_count = row_count // block_rows
    scalars = [challenge_limbs(challenges, position) for position in range(4)]
    shaped = (3, PAIRS, XSPLIT, YSPLIT, block_count, block_rows)
    select_blocks = jnp.transpose(selectors.reshape(shaped), (4, 0, 1, 2, 3, 5))
    proof_blocks = jnp.transpose(proofs.reshape(shaped), (4, 0, 1, 2, 3, 5))

    def one_block(tables):
        select_now, proof_now = tables
        points = []
        for round_index, position in enumerate([2, 2, 3, 3]):
            select_low, select_high = split_top(select_now, position)
            proof_low, proof_high = split_top(proof_now, position)
            points.append(round_points(select_low, select_high, proof_low, proof_high))
            select_now = fold_tables(select_low, select_high, scalars[round_index])
            proof_now = fold_tables(proof_low, proof_high, scalars[round_index])
        return jnp.stack(points, axis=1), select_now, proof_now

    points_all, select_done, proof_done = lax.map(one_block, (select_blocks, proof_blocks))
    summed = jnp.sum(points_all, axis=0)
    round_values = settle(summed[0], summed[1], summed[2])

    def arrange(done):
        rows_first = jnp.transpose(done, (1, 2, 3, 4, 0, 5)).reshape(3, PAIRS, XSPLIT // 4, YSPLIT // 4, row_count)
        blocks = rows_first.reshape(3, PAIRS, XSPLIT // 4, YSPLIT // 4, 4, 4, row_count // 16)
        return jnp.transpose(blocks, (0, 1, 4, 2, 5, 3, 6)).reshape(3, PAIRS, XSPLIT, YSPLIT, row_count // 16)

    return round_values, arrange(select_done), arrange(proof_done)
```

```python
import jax
import jax.numpy as jnp
from jax import lax
from jax.experimental import pallas as pl
from jax.experimental.pallas import tpu as pltpu
from jax.sharding import PartitionSpec as P

MESH = pl.DeviceIdType.MESH
I32 = jnp.int32
F32 = jnp.float32
MODULUS = 0x7FFFFFFF
STEPS = 8
TILES = 16
PART = 4


def srl(x, n):
    return lax.shift_right_logical(x, jnp.full(x.shape, n, I32))


def fold31(x):
    return (x & MODULUS) + srl(x, 31)


def encode(v):
    scaled = lax.shift_left((v & 0x7FFFFF) | 0x800000, srl(v, 23) & 7)
    power = lax.shift_left(jnp.full(v.shape, 1, I32), srl(v, 26) & 15).astype(F32)
    power = power * power
    power = power * power
    power = power * power
    unit = jnp.where(v >= 1 << 30, F32(-(2.0**-60)), F32(2.0**-60))
    return scaled.astype(F32) * unit * power


def decode(x):
    negative = x < 0
    a = jnp.abs(x)
    high = a >= F32(2.0**27)
    v = jnp.where(high, I32((1 << 29) - (1 << 23)), I32(-(1 << 23)))
    a = a * jnp.where(high, F32(2.0**-4), F32(2.0**60))
    for bit, shift in ((28, 32), (27, 16), (26, 8)):
        high = a >= F32(2.0 ** (23 + shift))
        v = v + jnp.where(high, I32(1 << bit), I32(0))
        a = a * jnp.where(high, F32(2.0**-shift), F32(1.0))
    v = v + jnp.where(negative, I32(1 << 30), I32(0))
    scaled = a.astype(I32)
    low = 8 - lax.clz(scaled)
    return v + lax.shift_right_logical(scaled, low) + lax.shift_left(low, jnp.full(low.shape, 23, I32))


def split(v):
    return v & 0xFFFF, srl(v, 16)


def difference(a, b):
    d = a - b
    return jnp.where(d < 0, d + MODULUS, d)


def add_product(sums, a, b):
    low = a[0] * b[0]
    middle = a[0] * b[1] + a[1] * b[0]
    high = (a[1] + a[1]) * b[1]
    return (
        sums[0] + ((low & 0xFFFF) + srl(middle, 15) + (high & 0xFFFF)),
        sums[1] + (srl(low, 16) + (middle & 0x7FFF) + srl(high, 16)),
    )


def folded(base, d, scalar):
    low = d[0] * scalar[0]
    middle = d[0] * scalar[1] + d[1] * scalar[0]
    t = fold31(low) + srl(middle, 15)
    t = fold31(t + d[1] * scalar[2])
    t = fold31(t + lax.shift_left(middle & 0x7FFF, jnp.full(middle.shape, 16, I32)))
    return fold31(t + base)


def two_rounds(selects, proofs, sums, scalars):
    select_parts, proof_parts = [split(v) for v in selects], [split(v) for v in proofs]
    sums = list(sums)
    for i in range(4):
        sums[i] = add_product(sums[i], select_parts[i], proof_parts[i])
    select_next, proof_next = [], []
    for pair in range(2):
        ds = split(difference(selects[2 * pair + 1], selects[2 * pair]))
        dp = split(difference(proofs[2 * pair + 1], proofs[2 * pair]))
        sums[4] = add_product(sums[4], ds, dp)
        select_next.append(folded(selects[2 * pair], ds, scalars[pair]))
        proof_next.append(folded(proofs[2 * pair], dp, scalars[pair]))
    for i in range(2):
        sums[5 + i] = add_product(sums[5 + i], split(select_next[i]), split(proof_next[i]))
    ds = split(difference(select_next[1], select_next[0]))
    dp = split(difference(proof_next[1], proof_next[0]))
    sums[7] = add_product(sums[7], ds, dp)
    return folded(select_next[0], ds, scalars[2]), folded(proof_next[0], dp, scalars[2]), tuple(sums)


def scalar_parts(challenge, flipped):
    other = 1 - challenge
    other = other + (lax.shift_right_arithmetic(other, I32(31)) & MODULUS)
    value = challenge * (1 - flipped) + other * flipped
    low, high = value & 0xFFFF, lax.shift_right_logical(value, I32(16))
    return [jnp.full((8, 128), s, I32) for s in (low, high, high + high)]


def across_tile(x):
    for shift in (64, 32, 16, 8, 4, 2, 1):
        x = x + pltpu.roll(x, shift, 1)
    return x


def kernel(
    challenges, selectors, proofs, out_points, out_selects, out_proofs,
    raw, y_send, y_recv, x_own, x_send, x_recv, sums_ref, done, gathered, gathered_z, tile_out,
    raw_sem, y_send_sem, y_recv_sem, x_send_sem, x_recv_sem, plane_send_sem, plane_recv_sem, z_send_sem, z_recv_sem, out_sem,
):
    gx, gy = lax.axis_index("gx"), lax.axis_index("gy")
    y, z_low = gx // 2, gx % 2
    x, z_core = gy // 4, gy % 4

    def plane_peer(dy, dx):
        return {"gx": (y + dy) % 4 * 2 + z_low, "gy": (x + dx) % 4 * 4 + z_core}

    def z_peer(m):
        z_high, core = z_core // 2, z_core % 2
        return {
            "gx": y * 2 + (z_low + m % 2) % 2,
            "gy": x * 4 + (z_high + m // 2 % 2) % 2 * 2 + (core + m // 4) % 2,
        }

    def load(step, table):
        source = (selectors, proofs)[table]
        return pltpu.make_async_copy(source.at[:, step], raw.at[step, table], raw_sem.at[step, table])

    def y_copy(step, k):
        return pltpu.make_async_remote_copy(
            y_send.at[step, k], y_recv.at[step, k], y_send_sem.at[step, k], y_recv_sem.at[step, k],
            device_id=plane_peer(k + 1, 0), device_id_type=MESH,
        )

    def x_copy(step, k):
        return pltpu.make_async_remote_copy(
            x_send.at[step, k], x_recv.at[step, k], x_send_sem.at[step, k], x_recv_sem.at[step, k],
            device_id=plane_peer(0, k + 1), device_id_type=MESH,
        )

    barrier = pltpu.get_barrier_semaphore()
    for m in range(1, 16):
        pl.semaphore_signal(barrier, 1, device_id=plane_peer(m // 4, m % 4), device_id_type=MESH)
    for m in range(1, 8):
        pl.semaphore_signal(barrier, 1, device_id=z_peer(m), device_id_type=MESH)

    for step in range(STEPS):
        for table in range(2):
            load(step, table).start()

    def raw_value(step, table, tile):
        low, middle, high = (raw[step, table, limb, tile].astype(I32) for limb in range(3))
        return low + lax.shift_left(middle, jnp.full(low.shape, 11, I32)) + lax.shift_left(high, jnp.full(low.shape, 22, I32))

    def prepare(step):
        for table in range(2):
            load(step, table).wait()

        def body(i, carry):
            k, t = i // TILES, i % TILES
            tile = (y + k + 1) % 4 * TILES + t
            for table in range(2):
                y_send[step, k, table, t] = encode(raw_value(step, table, tile))
            return carry

        lax.fori_loop(0, 3 * TILES, body, 0)

    def send(step):
        for k in range(3):
            y_copy(step, k).start()

    prepare(0)
    pl.semaphore_wait(barrier, 22)
    send(0)

    def ahead(step, carry):
        prepare(step)
        send(step)
        return carry

    lax.fori_loop(1, STEPS, ahead, 0)

    sums_ref[...] = jnp.zeros_like(sums_ref)

    def phase_scalars(position, first, second):
        behind = (position + 3) % 4
        return [
            scalar_parts(challenges[first], position // 2),
            scalar_parts(challenges[first], behind // 2),
            scalar_parts(challenges[second], position % 2),
        ]

    def load_sums(phase):
        return tuple((sums_ref[phase, i, 0], sums_ref[phase, i, 1]) for i in range(8))

    def store_sums(phase, sums):
        for i in range(8):
            for part in range(2):
                sums_ref[phase, i, part] = sums[i][part]

    y_scalars = phase_scalars(y, 0, 1)
    x_scalars = phase_scalars(x, 2, 3)

    def y_phase(step):
        for k in range(3):
            y_copy(step, k).wait_recv()

        def body(i, sums):
            part, t = i // PART, i % PART
            tile = (x + part) % 4 * PART + t
            tables = [
                [raw_value(step, table, y * TILES + tile)]
                + [decode(y_recv[step, k, table, tile]) for k in (1, 0, 2)]
                for table in range(2)
            ]
            select, proof, sums = two_rounds(tables[0], tables[1], sums, y_scalars)
            x_own[0, i], x_own[1, i] = select, proof
            return sums

        store_sums(0, lax.fori_loop(0, TILES, body, load_sums(0)))

        def coded(i, carry):
            k, t = i // PART, i % PART
            for table in range(2):
                x_send[step, k, table, t] = encode(x_own[table, PART + i])
            return carry

        lax.fori_loop(0, 3 * PART, coded, 0)
        for k in range(3):
            x_copy(step, k).start()
        for t in range(PART):
            for table in range(2):
                x_own[table, TILES + step * PART + t] = x_own[table, t]

    def x_phase(step):
        for k in range(3):
            x_copy(step, k).wait_recv()

        def body(t, sums):
            tables = [
                [x_own[table, TILES + step * PART + t]] + [decode(x_recv[step, k, table, t]) for k in (1, 0, 2)]
                for table in range(2)
            ]
            select, proof, sums = two_rounds(tables[0], tables[1], sums, x_scalars)
            for table, value in ((0, select), (1, proof)):
                done[table, step, t] = jnp.where(value == MODULUS, 0, value)
            return sums

        store_sums(1, lax.fori_loop(0, PART, body, load_sums(1)))

    def main(step, carry):
        y_phase(step)

        @pl.when(step >= 1)
        def _():
            x_phase(step - 1)

        return carry

    lax.fori_loop(0, STEPS, main, 0)
    x_phase(STEPS - 1)

    outs = [
        pltpu.make_async_copy(done.at[table], (out_selects, out_proofs)[table], out_sem.at[table]) for table in range(2)
    ]
    for copy in outs:
        copy.start()

    row = lax.broadcasted_iota(I32, (8, 128), 0)
    lane = lax.broadcasted_iota(I32, (8, 128), 1)
    halves = [[jnp.zeros((8, 128), I32) for _ in range(2)] for _ in range(3)]
    for phase, position in ((0, y), (1, x)):
        own_high, behind_high, odd = position // 2, (position + 3) % 4 // 2, position % 2
        sums = load_sums(phase)
        points = []
        for part in range(2):
            own, ahead_two, behind, ahead_one, across, even_sum, odd_sum, across_next = (s[part] for s in sums)
            upper = own * own_high + ahead_two * (1 - own_high) + behind * behind_high + ahead_one * (1 - behind_high)
            lower = own + ahead_two + behind + ahead_one - upper
            second_upper = even_sum * odd + odd_sum * (1 - odd)
            second_lower = even_sum + odd_sum - second_upper
            points.append((lower, upper, across, second_lower, second_upper, across_next))
        for i in range(6):
            at_round, at_point = 2 * phase + i // 3, i % 3
            low, high = points[0][i], points[1][i]
            value = fold31(low + srl(high, 15) + lax.shift_left(high & 0x7FFF, jnp.full(high.shape, 16, I32)))
            for half, piece in enumerate(split(value)):
                for shift in (4, 2, 1):
                    piece = piece + pltpu.roll(piece, shift, 0)
                halves[at_point][half] += jnp.where(row == at_round, piece, 0)
    tile = jnp.zeros((8, 128), I32)
    for at_point in range(3):
        low, high = (across_tile(half) for half in halves[at_point])
        value = fold31(low + srl(high, 15))
        value = fold31(value + lax.shift_left(high & 0x7FFF, jnp.full(high.shape, 16, I32)))
        for limb, piece in enumerate((value & 2047, srl(value, 11) & 2047, srl(value, 22))):
            tile += jnp.where(lane == 3 * limb + at_point, piece, 0)
    tile_out[0] = tile.astype(F32)

    def plane_copy(m):
        return pltpu.make_async_remote_copy(
            tile_out.at[0], gathered.at[m], plane_send_sem.at[m], plane_recv_sem.at[m],
            device_id=plane_peer(m // 4, m % 4), device_id_type=MESH,
        )

    def z_copy(m):
        return pltpu.make_async_remote_copy(
            tile_out.at[1], gathered_z.at[m], z_send_sem.at[m], z_recv_sem.at[m],
            device_id=z_peer(m), device_id_type=MESH,
        )

    for m in range(1, 16):
        plane_copy(m).start()
    total = tile_out[0]
    for m in range(1, 16):
        plane_copy(m).wait_recv()
        total = total + gathered[m]
    tile_out[1] = total
    for m in range(1, 8):
        z_copy(m).start()
    for m in range(1, 8):
        z_copy(m).wait_recv()
        total = total + gathered_z[m]

    limbs = total.astype(I32)
    middle, high = pltpu.roll(limbs, 125, 1), pltpu.roll(limbs, 122, 1)
    value = limbs + lax.shift_left(middle, jnp.full(middle.shape, 11, I32))
    value = fold31(value + srl(high, 9))
    value = fold31(value + lax.shift_left(high & 511, jnp.full(high.shape, 22, I32)))
    at_zero, at_one = pltpu.roll(value, 2, 1), pltpu.roll(value, 1, 1)
    at_two = fold31(fold31(value + value) + fold31(at_one + at_one))
    at_two = fold31(at_two + (MODULUS - at_zero))
    value = jnp.where(lane == 2, at_two, value)
    value = jnp.where(value == MODULUS, 0, value)
    for limb, piece in enumerate((value & 2047, srl(value, 11) & 2047, srl(value, 22))):
        out_points[limb] = piece.astype(F32)[:4, :3]

    for copy in outs:
        copy.wait()

    def finish(step, carry):
        for k in range(3):
            y_copy(step, k).wait_send()
            x_copy(step, k).wait_send()
        return carry

    lax.fori_loop(0, STEPS, finish, 0)
    for m in range(1, 16):
        plane_copy(m).wait_send()
    for m in range(1, 8):
        z_copy(m).wait_send()


def shards(selectors, proofs, challenges):
    points, selects, proofs_done = pl.pallas_call(
        kernel,
        out_shape=(
            jax.ShapeDtypeStruct((3, 4, 3), F32),
            jax.ShapeDtypeStruct((STEPS, PART, 8, 128), I32),
            jax.ShapeDtypeStruct((STEPS, PART, 8, 128), I32),
        ),
        in_specs=[
            pl.BlockSpec(memory_space=pltpu.SMEM),
            pl.BlockSpec(memory_space=pltpu.HBM),
            pl.BlockSpec(memory_space=pltpu.HBM),
        ],
        out_specs=(
            pl.BlockSpec(memory_space=pltpu.VMEM),
            pl.BlockSpec(memory_space=pltpu.HBM),
            pl.BlockSpec(memory_space=pltpu.HBM),
        ),
        scratch_shapes=[
            pltpu.VMEM((STEPS, 2, 3, 64, 8, 128), F32),
            pltpu.VMEM((STEPS, 3, 2, TILES, 8, 128), F32),
            pltpu.VMEM((STEPS, 3, 2, TILES, 8, 128), F32),
            pltpu.VMEM((2, TILES + STEPS * PART, 8, 128), I32),
            pltpu.VMEM((STEPS, 3, 2, PART, 8, 128), F32),
            pltpu.VMEM((STEPS, 3, 2, PART, 8, 128), F32),
            pltpu.VMEM((2, 8, 2, 8, 128), I32),
            pltpu.VMEM((2, STEPS, PART, 8, 128), I32),
            pltpu.VMEM((16, 8, 128), F32),
            pltpu.VMEM((8, 8, 128), F32),
            pltpu.VMEM((2, 8, 128), F32),
            pltpu.SemaphoreType.DMA((STEPS, 2)),
            pltpu.SemaphoreType.DMA((STEPS, 3)),
            pltpu.SemaphoreType.DMA((STEPS, 3)),
            pltpu.SemaphoreType.DMA((STEPS, 3)),
            pltpu.SemaphoreType.DMA((STEPS, 3)),
            pltpu.SemaphoreType.DMA((16,)),
            pltpu.SemaphoreType.DMA((16,)),
            pltpu.SemaphoreType.DMA((8,)),
            pltpu.SemaphoreType.DMA((8,)),
            pltpu.SemaphoreType.DMA((2,)),
        ],
        compiler_params=pltpu.CompilerParams(collective_id=0, has_side_effects=True, vmem_limit_bytes=60 << 20),
        name="sumcheck",
    )(challenges, selectors.reshape(3, 8, 64, 8, 128), proofs.reshape(3, 8, 64, 8, 128))

    def limbs(values):
        values = jnp.broadcast_to(values.reshape(1, 8, 32, 128), (3, 8, 32, 128))
        place = lax.broadcasted_iota(I32, values.shape, 0)
        return (lax.shift_right_logical(values, 11 * place) & 2047).astype(F32).reshape(3, 8, 1, 1, 4096)

    return points, limbs(selects), limbs(proofs_done)


def solution(mesh):
    tables = P(None, None, "gx", "gy", None)
    return jax.shard_map(shards, mesh=mesh, in_specs=(tables, tables, P()), out_specs=(P(), tables, tables), check_vma=False)
```

```python
import jax
import jax.numpy as jnp
from jax import lax
from jax.experimental import pallas as pl
from jax.experimental.pallas import tpu as pltpu
from jax.sharding import PartitionSpec as P

MESH = pl.DeviceIdType.MESH
I32 = jnp.int32
F32 = jnp.float32
MODULUS = 0x7FFFFFFF
STEPS = 8
LAST = STEPS - 1
TILES = 16
PART = 4
NEAR = (1, 3, 4)


def srl(x, n):
    return lax.shift_right_logical(x, jnp.full(x.shape, n, I32))


def fold31(x):
    return (x & MODULUS) + srl(x, 31)


def encode(v):
    scaled = lax.shift_left((v & 0x7FFFFF) | 0x800000, srl(v, 23) & 7)
    power = lax.shift_left(jnp.full(v.shape, 1, I32), srl(v, 26) & 15).astype(F32)
    power = power * power
    power = power * power
    power = power * power
    unit = jnp.where(v >= 1 << 30, F32(-(2.0**-60)), F32(2.0**-60))
    return scaled.astype(F32) * unit * power


def decode(x):
    negative = x < 0
    a = jnp.abs(x)
    high = a >= F32(2.0**27)
    v = jnp.where(high, I32((1 << 29) - (1 << 23)), I32(-(1 << 23)))
    a = a * jnp.where(high, F32(2.0**-4), F32(2.0**60))
    for bit, shift in ((28, 32), (27, 16), (26, 8)):
        high = a >= F32(2.0 ** (23 + shift))
        v = v + jnp.where(high, I32(1 << bit), I32(0))
        a = a * jnp.where(high, F32(2.0**-shift), F32(1.0))
    v = v + jnp.where(negative, I32(1 << 30), I32(0))
    scaled = a.astype(I32)
    low = 8 - lax.clz(scaled)
    return v + lax.shift_right_logical(scaled, low) + lax.shift_left(low, jnp.full(low.shape, 23, I32))


def split(v):
    return v & 0xFFFF, srl(v, 16)


def difference(a, b):
    d = a - b
    return jnp.where(d < 0, d + MODULUS, d)


def add_product(sums, a, b):
    low = a[0] * b[0]
    middle = a[0] * b[1] + a[1] * b[0]
    high = (a[1] + a[1]) * b[1]
    return (
        sums[0] + ((low & 0xFFFF) + srl(middle, 15) + (high & 0xFFFF)),
        sums[1] + (srl(low, 16) + (middle & 0x7FFF) + srl(high, 16)),
    )


def folded(base, d, scalar):
    low = d[0] * scalar[0]
    middle = d[0] * scalar[1] + d[1] * scalar[0]
    t = fold31(low) + srl(middle, 15)
    t = fold31(t + d[1] * scalar[2])
    t = fold31(t + lax.shift_left(middle & 0x7FFF, jnp.full(middle.shape, 16, I32)))
    return fold31(t + base)


def two_rounds(selects, proofs, sums, scalars):
    select_parts, proof_parts = [split(v) for v in selects], [split(v) for v in proofs]
    sums = list(sums)
    for i in range(4):
        sums[i] = add_product(sums[i], select_parts[i], proof_parts[i])
    select_next, proof_next = [], []
    for pair in range(2):
        ds = split(difference(selects[2 * pair + 1], selects[2 * pair]))
        dp = split(difference(proofs[2 * pair + 1], proofs[2 * pair]))
        sums[4] = add_product(sums[4], ds, dp)
        select_next.append(folded(selects[2 * pair], ds, scalars[pair]))
        proof_next.append(folded(proofs[2 * pair], dp, scalars[pair]))
    for i in range(2):
        sums[5 + i] = add_product(sums[5 + i], split(select_next[i]), split(proof_next[i]))
    ds = split(difference(select_next[1], select_next[0]))
    dp = split(difference(proof_next[1], proof_next[0]))
    sums[7] = add_product(sums[7], ds, dp)
    return folded(select_next[0], ds, scalars[2]), folded(proof_next[0], dp, scalars[2]), tuple(sums)


def scalar_parts(challenge, flipped):
    other = 1 - challenge
    other = other + (lax.shift_right_arithmetic(other, I32(31)) & MODULUS)
    value = challenge * (1 - flipped) + other * flipped
    low, high = value & 0xFFFF, lax.shift_right_logical(value, I32(16))
    return [jnp.full((8, 128), s, I32) for s in (low, high, high + high)]


def across_tile(x):
    for shift in (64, 32, 16, 8, 4, 2, 1):
        x = x + pltpu.roll(x, shift, 1)
    return x


def kernel(
    challenges, selectors, proofs, out_points, out_selects, out_proofs,
    raw, own, y_send, y_recv, early_send, early_recv, x_own, x_send, x_recv, sums_ref, gathered, gathered_z, tile_out,
    raw_sem, y_send_sem, y_recv_sem, early_send_sem, early_recv_sem, x_send_sem, x_recv_sem,
    plane_send_sem, plane_recv_sem, z_send_sem, z_recv_sem, token_sem,
):
    gx, gy = lax.axis_index("gx"), lax.axis_index("gy")
    y, z_low = gx // 2, gx % 2
    x, z_core = gy // 4, gy % 4

    def plane_peer(dy, dx):
        return {"gx": (y + dy) % 4 * 2 + z_low, "gy": (x + dx) % 4 * 4 + z_core}

    def z_peer(m):
        z_high, core = z_core // 2, z_core % 2
        return {
            "gx": y * 2 + (z_low + m % 2) % 2,
            "gy": x * 4 + (z_high + m // 2 % 2) % 2 * 2 + (core + m // 4) % 2,
        }

    def load(step, table):
        source = (selectors, proofs)[table]
        return pltpu.make_async_copy(source.at[:, step], raw.at[step, table], raw_sem.at[step, table])

    def y_copy(step, k):
        return pltpu.make_async_remote_copy(
            y_send.at[step, k], y_recv.at[step, k], y_send_sem.at[step, k], y_recv_sem.at[step, k],
            device_id=plane_peer(k + 1, 0), device_id_type=MESH,
        )

    def x_copy(step, k):
        return pltpu.make_async_remote_copy(
            x_send.at[step, k], x_recv.at[step, k], x_send_sem.at[step, k], x_recv_sem.at[step, k],
            device_id=plane_peer(0, k + 1), device_id_type=MESH,
        )

    def early_copy(k):
        return pltpu.make_async_remote_copy(
            early_send.at[k], early_recv.at[k], early_send_sem.at[k], early_recv_sem.at[k],
            device_id=plane_peer(0, k + 1), device_id_type=MESH,
        )

    barrier = pltpu.get_barrier_semaphore()
    for m in range(1, 4):
        pl.semaphore_signal(barrier, 1, device_id=plane_peer(m, 0), device_id_type=MESH)
        pl.semaphore_signal(barrier, 1, device_id=plane_peer(0, m), device_id_type=MESH)
        pl.semaphore_signal(barrier, 1, device_id=z_peer(NEAR[m - 1]), device_id_type=MESH)

    def tokens(turn):
        for m in range(3):
            pl.semaphore_signal(token_sem.at[turn, m], 1, device_id=z_peer(NEAR[m]), device_id_type=MESH)

    def await_tokens(turn):
        for m in range(3):
            pl.semaphore_wait(token_sem.at[turn, m], 1)

    for step in range(STEPS):
        for table in range(2):
            load(step, table).start()

    def raw_value(step, table, tile):
        low, middle, high = (raw[step, table, limb, tile].astype(I32) for limb in range(3))
        return low + lax.shift_left(middle, jnp.full(low.shape, 11, I32)) + lax.shift_left(high, jnp.full(low.shape, 22, I32))

    def prepare(step):
        for table in range(2):
            load(step, table).wait()

        def body(i, carry):
            k, t = i // TILES, i % TILES
            tile = (y + k + 1) % 4 * TILES + t
            for table in range(2):
                y_send[step, k, table, t] = encode(raw_value(step, table, tile))
            return carry

        lax.fori_loop(0, 3 * TILES, body, 0)

        def mine(t, carry):
            for table in range(2):
                own[step, table, t] = encode(raw_value(step, table, y * TILES + t))
            return carry

        lax.fori_loop(0, TILES, mine, 0)

    def send(step):
        for k in range(3):
            y_copy(step, k).start()

    def ahead(step, carry):
        prepare(step)
        send(step)
        return carry

    def prepare_early():
        for table in range(2):
            load(LAST, table).wait()

        def body(i, carry):
            k, quarter, t = i // TILES, i % TILES // PART, i % PART
            tile = quarter * TILES + (x + k + 1) % 4 * PART + t
            for table in range(2):
                early_send[k, table, quarter, t] = encode(raw_value(LAST, table, tile))
            return carry

        lax.fori_loop(0, 3 * TILES, body, 0)
        for k in range(3):
            early_copy(k).start()

        def mine(i, carry):
            k, t = i // PART, i % PART
            for table in range(2):
                y_send[LAST, k, table, t] = encode(raw_value(LAST, table, (y + k + 1) % 4 * TILES + x * PART + t))
            return carry

        lax.fori_loop(0, 3 * PART, mine, 0)
        for t in range(PART):
            for table in range(2):
                own[LAST, table, t] = encode(raw_value(LAST, table, y * TILES + x * PART + t))

    def prepare_last():
        for k in range(3):
            early_copy(k).wait_recv()

        def body(i, carry):
            k, t = i // PART, i % PART
            for table in range(2):
                for d in range(3):
                    y_send[LAST, d, table, PART + i] = early_recv[k, table, (y + d + 1) % 4, t]
                own[LAST, table, PART + i] = early_recv[k, table, y, t]
            return carry

        lax.fori_loop(0, 3 * PART, body, 0)

    prepare(0)
    pl.semaphore_wait(barrier, 9)
    send(0)
    tokens(0)
    lax.fori_loop(1, 2, ahead, 0)
    prepare_early()
    lax.fori_loop(2, LAST, ahead, 0)
    await_tokens(0)
    tokens(1)
    prepare_last()
    send(LAST)

    sums_ref[...] = jnp.zeros_like(sums_ref)

    def phase_scalars(position, first, second):
        behind = (position + 3) % 4
        return [
            scalar_parts(challenges[first], position // 2),
            scalar_parts(challenges[first], behind // 2),
            scalar_parts(challenges[second], position % 2),
        ]

    def load_sums(phase):
        return tuple((sums_ref[phase, i, 0], sums_ref[phase, i, 1]) for i in range(8))

    def store_sums(phase, sums):
        for i in range(8):
            for part in range(2):
                sums_ref[phase, i, part] = sums[i][part]

    y_scalars = phase_scalars(y, 0, 1)
    x_scalars = phase_scalars(x, 2, 3)

    def y_phase(step):
        for k in range(3):
            y_copy(step, k).wait_recv()

        def body(i, sums):
            part, t = i // PART, i % PART
            tile = (x + part) % 4 * PART + t
            is_last = step // LAST
            tile = tile + (i - tile) * is_last
            tables = [
                [decode(own[step, table, tile])] + [decode(y_recv[step, k, table, tile]) for k in (1, 0, 2)]
                for table in range(2)
            ]
            select, proof, sums = two_rounds(tables[0], tables[1], sums, y_scalars)
            x_own[0, i], x_own[1, i] = select, proof
            return sums

        store_sums(0, lax.fori_loop(0, TILES, body, load_sums(0)))

        def coded(i, carry):
            k, t = i // PART, i % PART
            for table in range(2):
                x_send[step, k, table, t] = encode(x_own[table, PART + i])
            return carry

        lax.fori_loop(0, 3 * PART, coded, 0)

        @pl.when(step < LAST)
        def _():
            for k in range(3):
                x_copy(step, k).start()

        for t in range(PART):
            for table in range(2):
                x_own[table, TILES + step * PART + t] = x_own[table, t]

    def x_phase(step, received):
        def body(t, sums):
            tables = [
                [x_own[table, TILES + step * PART + t]] + [decode(received[step, k, table, t]) for k in (1, 0, 2)]
                for table in range(2)
            ]
            select, proof, sums = two_rounds(tables[0], tables[1], sums, x_scalars)
            for ref, value in ((out_selects, select), (out_proofs, proof)):
                ref[step, t] = jnp.where(value == MODULUS, 0, value)
            return sums

        store_sums(1, lax.fori_loop(0, PART, body, load_sums(1)))

    def main(step, carry):
        y_phase(step)

        @pl.when(step >= 1)
        def _():
            for k in range(3):
                x_copy(step - 1, k).wait_recv()
            x_phase(step - 1, x_recv)

        return carry

    lax.fori_loop(0, STEPS, main, 0)
    x_phase(LAST, x_send)

    row = lax.broadcasted_iota(I32, (8, 128), 0)
    lane = lax.broadcasted_iota(I32, (8, 128), 1)
    halves = [[jnp.zeros((8, 128), I32) for _ in range(2)] for _ in range(3)]
    for phase, position in ((0, y), (1, x)):
        own_high, behind_high, odd = position // 2, (position + 3) % 4 // 2, position % 2
        sums = load_sums(phase)
        points = []
        for part in range(2):
            own, ahead_two, behind, ahead_one, across, even_sum, odd_sum, across_next = (s[part] for s in sums)
            upper = own * own_high + ahead_two * (1 - own_high) + behind * behind_high + ahead_one * (1 - behind_high)
            lower = own + ahead_two + behind + ahead_one - upper
            second_upper = even_sum * odd + odd_sum * (1 - odd)
            second_lower = even_sum + odd_sum - second_upper
            points.append((lower, upper, across, second_lower, second_upper, across_next))
        for i in range(6):
            at_round, at_point = 2 * phase + i // 3, i % 3
            low, high = points[0][i], points[1][i]
            value = fold31(low + srl(high, 15) + lax.shift_left(high & 0x7FFF, jnp.full(high.shape, 16, I32)))
            for half, piece in enumerate(split(value)):
                for shift in (4, 2, 1):
                    piece = piece + pltpu.roll(piece, shift, 0)
                halves[at_point][half] += jnp.where(row == at_round, piece, 0)
    tile = jnp.zeros((8, 128), I32)
    for at_point in range(3):
        low, high = (across_tile(half) for half in halves[at_point])
        value = fold31(low + srl(high, 15))
        value = fold31(value + lax.shift_left(high & 0x7FFF, jnp.full(high.shape, 16, I32)))
        for limb, piece in enumerate((value & 2047, srl(value, 11) & 2047, srl(value, 22))):
            tile += jnp.where(lane == 3 * limb + at_point, piece, 0)
    tile_out[0] = tile.astype(F32)

    def plane_copy(m):
        return pltpu.make_async_remote_copy(
            tile_out.at[0], gathered.at[m], plane_send_sem.at[m], plane_recv_sem.at[m],
            device_id=plane_peer(m // 4, m % 4), device_id_type=MESH,
        )

    def z_copy(m):
        return pltpu.make_async_remote_copy(
            tile_out.at[1], gathered_z.at[m], z_send_sem.at[m], z_recv_sem.at[m],
            device_id=z_peer(m), device_id_type=MESH,
        )

    for m in range(1, 16):
        plane_copy(m).start()
    total = tile_out[0]
    for m in range(1, 16):
        plane_copy(m).wait_recv()
        total = total + gathered[m]
    tile_out[1] = total
    await_tokens(1)
    for m in range(1, 8):
        z_copy(m).start()
    for m in range(1, 8):
        z_copy(m).wait_recv()
        total = total + gathered_z[m]

    limbs = total.astype(I32)
    middle, high = pltpu.roll(limbs, 125, 1), pltpu.roll(limbs, 122, 1)
    value = limbs + lax.shift_left(middle, jnp.full(middle.shape, 11, I32))
    value = fold31(value + srl(high, 9))
    value = fold31(value + lax.shift_left(high & 511, jnp.full(high.shape, 22, I32)))
    at_zero, at_one = pltpu.roll(value, 2, 1), pltpu.roll(value, 1, 1)
    at_two = fold31(fold31(value + value) + fold31(at_one + at_one))
    at_two = fold31(at_two + (MODULUS - at_zero))
    value = jnp.where(lane == 2, at_two, value)
    value = jnp.where(value == MODULUS, 0, value)
    for limb, piece in enumerate((value & 2047, srl(value, 11) & 2047, srl(value, 22))):
        out_points[limb] = piece.astype(F32)[:4, :3]

    def finish(step, carry):
        for k in range(3):
            y_copy(step, k).wait_send()
            x_copy(step, k).wait_send()
        return carry

    lax.fori_loop(0, LAST, finish, 0)
    for k in range(3):
        y_copy(LAST, k).wait_send()
        early_copy(k).wait_send()
    for m in range(1, 16):
        plane_copy(m).wait_send()
    for m in range(1, 8):
        z_copy(m).wait_send()


def write(points, selects, proofs, out_points, out_selects, out_proofs):
    out_points[...] = points[...]
    for ints, out in ((selects, out_selects), (proofs, out_proofs)):
        v = ints[...]
        for limb, piece in enumerate((v & 2047, srl(v, 11) & 2047, srl(v, 22))):
            out[limb] = piece.astype(F32)


def shards(selectors, proofs, challenges):
    vmem = pl.BlockSpec(memory_space=pltpu.VMEM)
    ints = jax.ShapeDtypeStruct((STEPS, PART, 8, 128), I32)
    results = pl.pallas_call(
        kernel,
        out_shape=(jax.ShapeDtypeStruct((3, 4, 3), F32), ints, ints),
        in_specs=[
            pl.BlockSpec(memory_space=pltpu.SMEM),
            pl.BlockSpec(memory_space=pltpu.HBM),
            pl.BlockSpec(memory_space=pltpu.HBM),
        ],
        out_specs=(vmem, vmem, vmem),
        scratch_shapes=[
            pltpu.VMEM((STEPS, 2, 3, 64, 8, 128), F32),
            pltpu.VMEM((STEPS, 2, TILES, 8, 128), F32),
            pltpu.VMEM((STEPS, 3, 2, TILES, 8, 128), F32),
            pltpu.VMEM((STEPS, 3, 2, TILES, 8, 128), F32),
            pltpu.VMEM((3, 2, 4, PART, 8, 128), F32),
            pltpu.VMEM((3, 2, 4, PART, 8, 128), F32),
            pltpu.VMEM((2, TILES + STEPS * PART, 8, 128), I32),
            pltpu.VMEM((STEPS, 3, 2, PART, 8, 128), F32),
            pltpu.VMEM((STEPS, 3, 2, PART, 8, 128), F32),
            pltpu.VMEM((2, 8, 2, 8, 128), I32),
            pltpu.VMEM((16, 8, 128), F32),
            pltpu.VMEM((8, 8, 128), F32),
            pltpu.VMEM((2, 8, 128), F32),
            pltpu.SemaphoreType.DMA((STEPS, 2)),
            pltpu.SemaphoreType.DMA((STEPS, 3)),
            pltpu.SemaphoreType.DMA((STEPS, 3)),
            pltpu.SemaphoreType.DMA((3,)),
            pltpu.SemaphoreType.DMA((3,)),
            pltpu.SemaphoreType.DMA((STEPS, 3)),
            pltpu.SemaphoreType.DMA((STEPS, 3)),
            pltpu.SemaphoreType.DMA((16,)),
            pltpu.SemaphoreType.DMA((16,)),
            pltpu.SemaphoreType.DMA((8,)),
            pltpu.SemaphoreType.DMA((8,)),
            pltpu.SemaphoreType.REGULAR((2, 3)),
        ],
        compiler_params=pltpu.CompilerParams(collective_id=0, has_side_effects=True, vmem_limit_bytes=60 << 20),
        name="sumcheck",
    )(challenges, selectors.reshape(3, 8, 64, 8, 128), proofs.reshape(3, 8, 64, 8, 128))
    limbs = jax.ShapeDtypeStruct((3, STEPS, PART, 8, 128), F32)
    points, selects, proofs_done = pl.pallas_call(
        write,
        out_shape=(jax.ShapeDtypeStruct((3, 4, 3), F32), limbs, limbs),
        in_specs=[vmem, vmem, vmem],
        out_specs=(vmem, vmem, vmem),
        name="write_limbs",
    )(*results)
    return points, selects.reshape(3, 8, 1, 1, 4096), proofs_done.reshape(3, 8, 1, 1, 4096)


def solution(mesh):
    tables = P(None, None, "gx", "gy", None)
    return jax.shard_map(shards, mesh=mesh, in_specs=(tables, tables, P()), out_specs=(P(), tables, tables), check_vma=False)
```

```python
import jax
import jax.numpy as jnp
from jax import lax
from jax.experimental import pallas as pl
from jax.experimental.pallas import tpu as pltpu
from jax.sharding import PartitionSpec as P

MESH = pl.DeviceIdType.MESH
I32 = jnp.int32
F32 = jnp.float32
MODULUS = 0x7FFFFFFF
STEPS = 8
LAST = STEPS - 1
TILES = 16
PART = 4
FAR_FIRST = (10, 9, 11, 6, 14, 5, 7, 13, 15, 2, 8, 1, 3, 4, 12)
NEAR = (1, 3, 4)


def srl(x, n):
    return lax.shift_right_logical(x, jnp.full(x.shape, n, I32))


def fold31(x):
    return (x & MODULUS) + srl(x, 31)


def encode(v):
    scaled = lax.shift_left((v & 0x7FFFFF) | 0x800000, srl(v, 23) & 7)
    power = lax.shift_left(jnp.full(v.shape, 1, I32), srl(v, 26) & 15).astype(F32)
    power = power * power
    power = power * power
    power = power * power
    unit = jnp.where(v >= 1 << 30, F32(-(2.0**-60)), F32(2.0**-60))
    return scaled.astype(F32) * unit * power


def decode(x):
    negative = x < 0
    a = jnp.abs(x)
    high = a >= F32(2.0**27)
    v = jnp.where(high, I32((1 << 29) - (1 << 23)), I32(-(1 << 23)))
    a = a * jnp.where(high, F32(2.0**-4), F32(2.0**60))
    for bit, shift in ((28, 32), (27, 16), (26, 8)):
        high = a >= F32(2.0 ** (23 + shift))
        v = v + jnp.where(high, I32(1 << bit), I32(0))
        a = a * jnp.where(high, F32(2.0**-shift), F32(1.0))
    v = v + jnp.where(negative, I32(1 << 30), I32(0))
    scaled = a.astype(I32)
    low = 8 - lax.clz(scaled)
    return v + lax.shift_right_logical(scaled, low) + lax.shift_left(low, jnp.full(low.shape, 23, I32))


def split(v):
    return v & 0xFFFF, srl(v, 16)


def difference(a, b):
    d = a - b
    return jnp.where(d < 0, d + MODULUS, d)


def add_product(sums, a, b):
    low = a[0] * b[0]
    middle = a[0] * b[1] + a[1] * b[0]
    high = (a[1] + a[1]) * b[1]
    return (
        sums[0] + ((low & 0xFFFF) + srl(middle, 15) + (high & 0xFFFF)),
        sums[1] + (srl(low, 16) + (middle & 0x7FFF) + srl(high, 16)),
    )


def folded(base, d, scalar):
    low = d[0] * scalar[0]
    middle = d[0] * scalar[1] + d[1] * scalar[0]
    t = fold31(low) + srl(middle, 15)
    t = fold31(t + d[1] * scalar[2])
    t = fold31(t + lax.shift_left(middle & 0x7FFF, jnp.full(middle.shape, 16, I32)))
    return fold31(t + base)


def two_rounds(selects, proofs, sums, scalars):
    select_parts, proof_parts = [split(v) for v in selects], [split(v) for v in proofs]
    sums = list(sums)
    for i in range(4):
        sums[i] = add_product(sums[i], select_parts[i], proof_parts[i])
    select_next, proof_next = [], []
    for pair in range(2):
        ds = split(difference(selects[2 * pair + 1], selects[2 * pair]))
        dp = split(difference(proofs[2 * pair + 1], proofs[2 * pair]))
        sums[4] = add_product(sums[4], ds, dp)
        select_next.append(folded(selects[2 * pair], ds, scalars[pair]))
        proof_next.append(folded(proofs[2 * pair], dp, scalars[pair]))
    for i in range(2):
        sums[5 + i] = add_product(sums[5 + i], split(select_next[i]), split(proof_next[i]))
    ds = split(difference(select_next[1], select_next[0]))
    dp = split(difference(proof_next[1], proof_next[0]))
    sums[7] = add_product(sums[7], ds, dp)
    return folded(select_next[0], ds, scalars[2]), folded(proof_next[0], dp, scalars[2]), tuple(sums)


def scalar_parts(challenge, flipped):
    other = 1 - challenge
    other = other + (lax.shift_right_arithmetic(other, I32(31)) & MODULUS)
    value = challenge * (1 - flipped) + other * flipped
    low, high = value & 0xFFFF, lax.shift_right_logical(value, I32(16))
    return [jnp.full((8, 128), s, I32) for s in (low, high, high + high)]


def across_tile(x):
    for shift in (64, 32, 16, 8, 4, 2, 1):
        x = x + pltpu.roll(x, shift, 1)
    return x


def kernel(
    challenges_in, selectors, proofs, out_points, out_selects, out_proofs,
    raw, own, y_send, y_recv, early_send, early_recv, x_own, x_send, x_recv, sums_ref, gathered, gathered_z, tile_out, challenges,
    raw_sem, y_send_sem, y_recv_sem, early_send_sem, early_recv_sem, x_send_sem, x_recv_sem,
    last_send_sem, last_recv_sem, plane_send_sem, plane_recv_sem, z_send_sem, z_recv_sem, token_sem, challenge_sem,
):
    gx, gy = lax.axis_index("gx"), lax.axis_index("gy")
    y, z_low = gx // 2, gx % 2
    x, z_core = gy // 4, gy % 4

    def plane_peer(dy, dx):
        return {"gx": (y + dy) % 4 * 2 + z_low, "gy": (x + dx) % 4 * 4 + z_core}

    def z_peer(m):
        z_high, core = z_core // 2, z_core % 2
        return {
            "gx": y * 2 + (z_low + m % 2) % 2,
            "gy": x * 4 + (z_high + m // 2 % 2) % 2 * 2 + (core + m // 4) % 2,
        }

    def load(step, table):
        source = (selectors, proofs)[table]
        return pltpu.make_async_copy(source.at[:, step], raw.at[step, table], raw_sem.at[step, table])

    def y_copy(step, k):
        return pltpu.make_async_remote_copy(
            y_send.at[step, k], y_recv.at[step, k], y_send_sem.at[step, k], y_recv_sem.at[step, k],
            device_id=plane_peer(k + 1, 0), device_id_type=MESH,
        )

    def last_copy(t, k):
        return pltpu.make_async_remote_copy(
            y_send.at[LAST, k, :, pl.ds(4 * t, 4)], y_recv.at[LAST, k, :, pl.ds(4 * t, 4)],
            last_send_sem.at[t, k], last_recv_sem.at[t, k],
            device_id=plane_peer(k + 1, 0), device_id_type=MESH,
        )

    def x_copy(step, k):
        return pltpu.make_async_remote_copy(
            x_send.at[step, k], x_recv.at[step, k], x_send_sem.at[step, k], x_recv_sem.at[step, k],
            device_id=plane_peer(0, k + 1), device_id_type=MESH,
        )

    def early_copy(k):
        return pltpu.make_async_remote_copy(
            early_send.at[k], early_recv.at[k], early_send_sem.at[k], early_recv_sem.at[k],
            device_id=plane_peer(0, k + 1), device_id_type=MESH,
        )

    barrier = pltpu.get_barrier_semaphore()
    for m in range(1, 4):
        pl.semaphore_signal(barrier, 1, device_id=plane_peer(m, 0), device_id_type=MESH)
        pl.semaphore_signal(barrier, 1, device_id=plane_peer(0, m), device_id_type=MESH)
        pl.semaphore_signal(barrier, 1, device_id=z_peer(NEAR[m - 1]), device_id_type=MESH)

    def tokens(turn):
        for m in range(3):
            pl.semaphore_signal(token_sem.at[turn, m], 1, device_id=z_peer(NEAR[m]), device_id_type=MESH)

    def await_tokens(turn):
        for m in range(3):
            pl.semaphore_wait(token_sem.at[turn, m], 1)

    for step in range(STEPS):
        for table in range(2):
            load(step, table).start()
    challenge_copy = pltpu.make_async_copy(challenges_in, challenges, challenge_sem)
    challenge_copy.start()

    def raw_value(step, table, tile):
        low, middle, high = (raw[step, table, limb, tile].astype(I32) for limb in range(3))
        return low + lax.shift_left(middle, jnp.full(low.shape, 11, I32)) + lax.shift_left(high, jnp.full(low.shape, 22, I32))

    def prepare(step):
        for table in range(2):
            load(step, table).wait()

        def body(i, carry):
            k, t = i // TILES, i % TILES
            tile = (y + k + 1) % 4 * TILES + t
            for table in range(2):
                y_send[step, k, table, t] = encode(raw_value(step, table, tile))
            return carry

        lax.fori_loop(0, 3 * TILES, body, 0)

        def mine(t, carry):
            for table in range(2):
                own[step, table, t] = encode(raw_value(step, table, y * TILES + t))
            return carry

        lax.fori_loop(0, TILES, mine, 0)

    def send(step):
        for k in range(3):
            y_copy(step, k).start()

    def ahead(step, carry):
        prepare(step)
        send(step)
        return carry

    def prepare_early():
        for table in range(2):
            load(LAST, table).wait()

        def body(i, carry):
            k, quarter, t = i // TILES, i % TILES // PART, i % PART
            tile = quarter * TILES + (x + k + 1) % 4 * PART + t
            for table in range(2):
                early_send[k, table, quarter, t] = encode(raw_value(LAST, table, tile))
            return carry

        lax.fori_loop(0, 3 * TILES, body, 0)
        for k in range(3):
            early_copy(k).start()

        def mine(i, carry):
            k, t = i // PART, i % PART
            for table in range(2):
                y_send[LAST, k, table, 4 * t] = encode(raw_value(LAST, table, (y + k + 1) % 4 * TILES + x * PART + t))
            return carry

        lax.fori_loop(0, 3 * PART, mine, 0)
        for t in range(PART):
            for table in range(2):
                own[LAST, table, 4 * t] = encode(raw_value(LAST, table, y * TILES + x * PART + t))

    def prepare_last():
        for k in range(3):
            early_copy(k).wait_recv()

        def body(i, carry):
            k, t = i // PART, i % PART
            for table in range(2):
                for d in range(3):
                    y_send[LAST, d, table, 4 * t + k + 1] = early_recv[k, table, (y + d + 1) % 4, t]
                own[LAST, table, 4 * t + k + 1] = early_recv[k, table, y, t]
            return carry

        lax.fori_loop(0, 3 * PART, body, 0)

    prepare(0)
    pl.semaphore_wait(barrier, 9)
    send(0)
    tokens(0)
    lax.fori_loop(1, 2, ahead, 0)
    prepare_early()
    lax.fori_loop(2, LAST, ahead, 0)
    await_tokens(0)
    tokens(1)
    prepare_last()
    for t in range(PART):
        for k in range(3):
            last_copy(t, k).start()

    sums_ref[...] = jnp.zeros_like(sums_ref)

    def phase_scalars(position, first, second):
        behind = (position + 3) % 4
        return [
            scalar_parts(challenges[first], position // 2),
            scalar_parts(challenges[first], behind // 2),
            scalar_parts(challenges[second], position % 2),
        ]

    def load_sums(phase):
        return tuple((sums_ref[phase, i, 0], sums_ref[phase, i, 1]) for i in range(8))

    def store_sums(phase, sums):
        for i in range(8):
            for part in range(2):
                sums_ref[phase, i, part] = sums[i][part]

    challenge_copy.wait()
    y_scalars = phase_scalars(y, 0, 1)
    x_scalars = phase_scalars(x, 2, 3)

    def y_phase(step):
        for k in range(3):
            y_copy(step, k).wait_recv()

        def body(i, sums):
            part, t = i // PART, i % PART
            tile = (x + part) % 4 * PART + t
            tables = [
                [decode(own[step, table, tile])] + [decode(y_recv[step, k, table, tile]) for k in (1, 0, 2)]
                for table in range(2)
            ]
            select, proof, sums = two_rounds(tables[0], tables[1], sums, y_scalars)
            x_own[0, i], x_own[1, i] = select, proof
            return sums

        store_sums(0, lax.fori_loop(0, TILES, body, load_sums(0)))

        def coded(i, carry):
            k, t = i // PART, i % PART
            for table in range(2):
                x_send[step, k, table, t] = encode(x_own[table, PART + i])
            return carry

        lax.fori_loop(0, 3 * PART, coded, 0)

        for k in range(3):
            x_copy(step, k).start()
        for t in range(PART):
            for table in range(2):
                x_own[table, TILES + step * PART + t] = x_own[table, t]

    def finished(step, t, select, proof):
        for ref, value in ((out_selects, select), (out_proofs, proof)):
            ref[step, t] = jnp.where(value == MODULUS, 0, value)

    def x_phase(step):
        for k in range(3):
            x_copy(step, k).wait_recv()

        def body(t, sums):
            tables = [
                [x_own[table, TILES + step * PART + t]] + [decode(x_recv[step, k, table, t]) for k in (1, 0, 2)]
                for table in range(2)
            ]
            select, proof, sums = two_rounds(tables[0], tables[1], sums, x_scalars)
            finished(step, t, select, proof)
            return sums

        store_sums(1, lax.fori_loop(0, PART, body, load_sums(1)))

    def last_phase(t):
        for k in range(3):
            last_copy(t, k).wait_recv()

        def body(r, sums):
            tables = [
                [decode(own[LAST, table, 4 * t + r])] + [decode(y_recv[LAST, k, table, 4 * t + r]) for k in (1, 0, 2)]
                for table in range(2)
            ]
            x_own[0, r], x_own[1, r], sums = two_rounds(tables[0], tables[1], sums, y_scalars)
            return sums

        store_sums(0, lax.fori_loop(0, 4, body, load_sums(0)))
        tables = [[x_own[table, r] for r in (0, 2, 1, 3)] for table in range(2)]
        select, proof, sums = two_rounds(tables[0], tables[1], load_sums(1), x_scalars)
        store_sums(1, sums)
        finished(LAST, t, select, proof)

    def main(step, carry):
        y_phase(step)

        @pl.when(step >= 1)
        def _():
            x_phase(step - 1)

        return carry

    lax.fori_loop(0, LAST, main, 0)

    def last(t, carry):
        last_phase(t)

        @pl.when(t == 2)
        def _():
            x_phase(LAST - 1)

        return carry

    lax.fori_loop(0, PART, last, 0)

    row = lax.broadcasted_iota(I32, (8, 128), 0)
    lane = lax.broadcasted_iota(I32, (8, 128), 1)
    halves = [[jnp.zeros((8, 128), I32) for _ in range(2)] for _ in range(3)]
    for phase, position in ((0, y), (1, x)):
        own_high, behind_high, odd = position // 2, (position + 3) % 4 // 2, position % 2
        sums = load_sums(phase)
        points = []
        for part in range(2):
            own, ahead_two, behind, ahead_one, across, even_sum, odd_sum, across_next = (s[part] for s in sums)
            upper = own * own_high + ahead_two * (1 - own_high) + behind * behind_high + ahead_one * (1 - behind_high)
            lower = own + ahead_two + behind + ahead_one - upper
            second_upper = even_sum * odd + odd_sum * (1 - odd)
            second_lower = even_sum + odd_sum - second_upper
            points.append((lower, upper, across, second_lower, second_upper, across_next))
        for i in range(6):
            at_round, at_point = 2 * phase + i // 3, i % 3
            low, high = points[0][i], points[1][i]
            value = fold31(low + srl(high, 15) + lax.shift_left(high & 0x7FFF, jnp.full(high.shape, 16, I32)))
            for half, piece in enumerate(split(value)):
                for shift in (4, 2, 1):
                    piece = piece + pltpu.roll(piece, shift, 0)
                halves[at_point][half] += jnp.where(row == at_round, piece, 0)
    tile = jnp.zeros((8, 128), I32)
    for at_point in range(3):
        low, high = (across_tile(half) for half in halves[at_point])
        value = fold31(low + srl(high, 15))
        value = fold31(value + lax.shift_left(high & 0x7FFF, jnp.full(high.shape, 16, I32)))
        for limb, piece in enumerate((value & 2047, srl(value, 11) & 2047, srl(value, 22))):
            tile += jnp.where(lane == 3 * limb + at_point, piece, 0)
    tile_out[0] = tile.astype(F32)

    def plane_copy(m):
        return pltpu.make_async_remote_copy(
            tile_out.at[1], gathered.at[m], plane_send_sem.at[m], plane_recv_sem.at[m],
            device_id=plane_peer(m // 4, m % 4), device_id_type=MESH,
        )

    def z_copy(m):
        return pltpu.make_async_remote_copy(
            tile_out.at[0], gathered_z.at[m], z_send_sem.at[m], z_recv_sem.at[m],
            device_id=z_peer(m), device_id_type=MESH,
        )

    await_tokens(1)
    for m in range(1, 8):
        z_copy(m).start()

    def finish(step, carry):
        for k in range(3):
            y_copy(step, k).wait_send()
            x_copy(step, k).wait_send()
        return carry

    lax.fori_loop(0, LAST, finish, 0)
    for k in range(3):
        early_copy(k).wait_send()
        for t in range(PART):
            last_copy(t, k).wait_send()
    total = tile_out[0]
    for m in range(1, 8):
        z_copy(m).wait_recv()
        total = total + gathered_z[m]
    tile_out[1] = total
    for m in FAR_FIRST:
        plane_copy(m).start()
    for m in range(1, 8):
        z_copy(m).wait_send()
    for m in range(1, 16):
        plane_copy(m).wait_recv()
        total = total + gathered[m]

    limbs = total.astype(I32)
    middle, high = pltpu.roll(limbs, 125, 1), pltpu.roll(limbs, 122, 1)
    value = limbs + lax.shift_left(middle, jnp.full(middle.shape, 11, I32))
    value = fold31(value + srl(high, 9))
    value = fold31(value + lax.shift_left(high & 511, jnp.full(high.shape, 22, I32)))
    at_zero, at_one = pltpu.roll(value, 2, 1), pltpu.roll(value, 1, 1)
    at_two = fold31(fold31(value + value) + fold31(at_one + at_one))
    at_two = fold31(at_two + (MODULUS - at_zero))
    value = jnp.where(lane == 2, at_two, value)
    value = jnp.where(value == MODULUS, 0, value)
    for limb, piece in enumerate((value & 2047, srl(value, 11) & 2047, srl(value, 22))):
        out_points[limb] = piece.astype(F32)[:4, :3]

    for m in range(1, 16):
        plane_copy(m).wait_send()


def write(points, selects, proofs, out_points, out_selects, out_proofs):
    out_points[...] = points[...]
    for ints, out in ((selects, out_selects), (proofs, out_proofs)):
        v = ints[...]
        for limb, piece in enumerate((v & 2047, srl(v, 11) & 2047, srl(v, 22))):
            out[limb] = piece.astype(F32)


def shards(selectors, proofs, challenges):
    vmem = pl.BlockSpec(memory_space=pltpu.VMEM)
    tables = [t.reshape(3, 8, 64, 8, 128) for t in (selectors, proofs)]
    ints = pltpu.VMEM((STEPS, PART, 8, 128), I32)
    results = pl.pallas_call(
        kernel,
        out_shape=(pltpu.VMEM((3, 4, 3), F32), ints, ints),
        in_specs=[
            pl.BlockSpec(memory_space=pltpu.HBM),
            pl.BlockSpec(memory_space=pltpu.HBM),
            pl.BlockSpec(memory_space=pltpu.HBM),
        ],
        out_specs=(vmem, vmem, vmem),
        scratch_shapes=[
            pltpu.VMEM((STEPS, 2, 3, 64, 8, 128), F32),
            pltpu.VMEM((STEPS, 2, TILES, 8, 128), F32),
            pltpu.VMEM((STEPS, 3, 2, TILES, 8, 128), F32),
            pltpu.VMEM((STEPS, 3, 2, TILES, 8, 128), F32),
            pltpu.VMEM((3, 2, 4, PART, 8, 128), F32),
            pltpu.VMEM((3, 2, 4, PART, 8, 128), F32),
            pltpu.VMEM((2, TILES + STEPS * PART, 8, 128), I32),
            pltpu.VMEM((STEPS, 3, 2, PART, 8, 128), F32),
            pltpu.VMEM((STEPS, 3, 2, PART, 8, 128), F32),
            pltpu.VMEM((2, 8, 2, 8, 128), I32),
            pltpu.VMEM((16, 8, 128), F32),
            pltpu.VMEM((8, 8, 128), F32),
            pltpu.VMEM((2, 8, 128), F32),
            pltpu.SMEM((4,), I32),
            pltpu.SemaphoreType.DMA((STEPS, 2)),
            pltpu.SemaphoreType.DMA((STEPS, 3)),
            pltpu.SemaphoreType.DMA((STEPS, 3)),
            pltpu.SemaphoreType.DMA((3,)),
            pltpu.SemaphoreType.DMA((3,)),
            pltpu.SemaphoreType.DMA((STEPS, 3)),
            pltpu.SemaphoreType.DMA((STEPS, 3)),
            pltpu.SemaphoreType.DMA((PART, 3)),
            pltpu.SemaphoreType.DMA((PART, 3)),
            pltpu.SemaphoreType.DMA((16,)),
            pltpu.SemaphoreType.DMA((16,)),
            pltpu.SemaphoreType.DMA((8,)),
            pltpu.SemaphoreType.DMA((8,)),
            pltpu.SemaphoreType.REGULAR((2, 3)),
            pltpu.SemaphoreType.DMA,
        ],
        compiler_params=pltpu.CompilerParams(collective_id=0, has_side_effects=True, vmem_limit_bytes=40 << 20),
        name="sumcheck",
    )(*(pltpu.with_memory_space_constraint(t, pltpu.HBM) for t in (challenges, *tables)))
    limbs = jax.ShapeDtypeStruct((3, STEPS, PART, 8, 128), F32)
    points, selects, proofs_done = pl.pallas_call(
        write,
        out_shape=(jax.ShapeDtypeStruct((3, 4, 3), F32), limbs, limbs),
        in_specs=[vmem, vmem, vmem],
        out_specs=(vmem, vmem, vmem),
        name="write_limbs",
    )(*(pltpu.with_memory_space_constraint(r, pltpu.VMEM) for r in results))
    return points, selects.reshape(3, 8, 1, 1, 4096), proofs_done.reshape(3, 8, 1, 1, 4096)


def solution(mesh):
    tables = P(None, None, "gx", "gy", None)
    return jax.shard_map(shards, mesh=mesh, in_specs=(tables, tables, P()), out_specs=(P(), tables, tables), check_vma=False)
```

```python
import jax
import jax.numpy as jnp
from jax import lax
from jax.experimental import pallas as pl
from jax.experimental.pallas import tpu as pltpu
from jax.sharding import PartitionSpec as P

MESH = pl.DeviceIdType.MESH
I32 = jnp.int32
F32 = jnp.float32
MODULUS = 0x7FFFFFFF
STEPS = 8
EARLY = 2
LATE = STEPS - EARLY
TILES = 16
PART = 4
FAR_FIRST = (10, 9, 11, 6, 14, 5, 7, 13, 15, 2, 8, 1, 3, 4, 12)
NEAR = (1, 3, 4)


def srl(x, n):
    return lax.shift_right_logical(x, jnp.full(x.shape, n, I32))


def fold31(x):
    return (x & MODULUS) + srl(x, 31)


def encode(v):
    scaled = lax.shift_left((v & 0x7FFFFF) | 0x800000, srl(v, 23) & 7)
    power = lax.shift_left(jnp.full(v.shape, 1, I32), srl(v, 26) & 15).astype(F32)
    power = power * power
    power = power * power
    power = power * power
    unit = jnp.where(v >= 1 << 30, F32(-(2.0**-60)), F32(2.0**-60))
    return scaled.astype(F32) * unit * power


def decode(x):
    negative = x < 0
    a = jnp.abs(x)
    high = a >= F32(2.0**27)
    v = jnp.where(high, I32((1 << 29) - (1 << 23)), I32(-(1 << 23)))
    a = a * jnp.where(high, F32(2.0**-4), F32(2.0**60))
    for bit, shift in ((28, 32), (27, 16), (26, 8)):
        high = a >= F32(2.0 ** (23 + shift))
        v = v + jnp.where(high, I32(1 << bit), I32(0))
        a = a * jnp.where(high, F32(2.0**-shift), F32(1.0))
    v = v + jnp.where(negative, I32(1 << 30), I32(0))
    scaled = a.astype(I32)
    low = 8 - lax.clz(scaled)
    return v + lax.shift_right_logical(scaled, low) + lax.shift_left(low, jnp.full(low.shape, 23, I32))


def split(v):
    return v & 0xFFFF, srl(v, 16)


def difference(a, b):
    d = a - b
    return jnp.where(d < 0, d + MODULUS, d)


def add_product(sums, a, b):
    low = a[0] * b[0]
    middle = a[0] * b[1] + a[1] * b[0]
    high = (a[1] + a[1]) * b[1]
    return (
        sums[0] + ((low & 0xFFFF) + srl(middle, 15) + (high & 0xFFFF)),
        sums[1] + (srl(low, 16) + (middle & 0x7FFF) + srl(high, 16)),
    )


def folded(base, d, scalar):
    low = d[0] * scalar[0]
    middle = d[0] * scalar[1] + d[1] * scalar[0]
    t = fold31(low) + srl(middle, 15)
    t = fold31(t + d[1] * scalar[2])
    t = fold31(t + lax.shift_left(middle & 0x7FFF, jnp.full(middle.shape, 16, I32)))
    return fold31(t + base)


def two_rounds(selects, proofs, sums, scalars):
    select_parts, proof_parts = [split(v) for v in selects], [split(v) for v in proofs]
    sums = list(sums)
    for i in range(4):
        sums[i] = add_product(sums[i], select_parts[i], proof_parts[i])
    select_next, proof_next = [], []
    for pair in range(2):
        ds = split(difference(selects[2 * pair + 1], selects[2 * pair]))
        dp = split(difference(proofs[2 * pair + 1], proofs[2 * pair]))
        sums[4] = add_product(sums[4], ds, dp)
        select_next.append(folded(selects[2 * pair], ds, scalars[pair]))
        proof_next.append(folded(proofs[2 * pair], dp, scalars[pair]))
    for i in range(2):
        sums[5 + i] = add_product(sums[5 + i], split(select_next[i]), split(proof_next[i]))
    ds = split(difference(select_next[1], select_next[0]))
    dp = split(difference(proof_next[1], proof_next[0]))
    sums[7] = add_product(sums[7], ds, dp)
    return folded(select_next[0], ds, scalars[2]), folded(proof_next[0], dp, scalars[2]), tuple(sums)


def scalar_parts(challenge, flipped):
    other = 1 - challenge
    other = other + (lax.shift_right_arithmetic(other, I32(31)) & MODULUS)
    value = challenge * (1 - flipped) + other * flipped
    low, high = value & 0xFFFF, lax.shift_right_logical(value, I32(16))
    return [jnp.full((8, 128), s, I32) for s in (low, high, high + high)]


def across_tile(x):
    for shift in (64, 32, 16, 8, 4, 2, 1):
        x = x + pltpu.roll(x, shift, 1)
    return x


def kernel(
    challenges_in, selectors, proofs, out_points, out_selects, out_proofs,
    raw, own, y_send, y_recv, early_send, early_recv, x_own, x_send, x_recv, sums_ref, gathered, gathered_z, tile_out, challenges,
    raw_sem, y_send_sem, y_recv_sem, early_send_sem, early_recv_sem, x_send_sem, x_recv_sem,
    last_send_sem, last_recv_sem, plane_send_sem, plane_recv_sem, z_send_sem, z_recv_sem, token_sem, challenge_sem,
):
    gx, gy = lax.axis_index("gx"), lax.axis_index("gy")
    y, z_low = gx // 2, gx % 2
    x, z_core = gy // 4, gy % 4

    def plane_peer(dy, dx):
        return {"gx": (y + dy) % 4 * 2 + z_low, "gy": (x + dx) % 4 * 4 + z_core}

    def z_peer(m):
        z_high, core = z_core // 2, z_core % 2
        return {
            "gx": y * 2 + (z_low + m % 2) % 2,
            "gy": x * 4 + (z_high + m // 2 % 2) % 2 * 2 + (core + m // 4) % 2,
        }

    def load(step, table):
        source = (selectors, proofs)[table]
        return pltpu.make_async_copy(source.at[:, step], raw.at[step, table], raw_sem.at[step, table])

    def y_copy(step, k):
        return pltpu.make_async_remote_copy(
            y_send.at[step, k], y_recv.at[step, k], y_send_sem.at[step, k], y_recv_sem.at[step, k],
            device_id=plane_peer(k + 1, 0), device_id_type=MESH,
        )

    def last_copy(e, t, k):
        return pltpu.make_async_remote_copy(
            y_send.at[LATE + e, k, :, pl.ds(4 * t, 4)], y_recv.at[LATE + e, k, :, pl.ds(4 * t, 4)],
            last_send_sem.at[e, t, k], last_recv_sem.at[e, t, k],
            device_id=plane_peer(k + 1, 0), device_id_type=MESH,
        )

    def x_copy(step, k):
        return pltpu.make_async_remote_copy(
            x_send.at[step, k], x_recv.at[step, k], x_send_sem.at[step, k], x_recv_sem.at[step, k],
            device_id=plane_peer(0, k + 1), device_id_type=MESH,
        )

    def early_copy(e, k):
        return pltpu.make_async_remote_copy(
            early_send.at[e, k], early_recv.at[e, k], early_send_sem.at[e, k], early_recv_sem.at[e, k],
            device_id=plane_peer(0, k + 1), device_id_type=MESH,
        )

    gathered[...] = jnp.zeros_like(gathered)
    gathered_z[...] = jnp.zeros_like(gathered_z)

    barrier = pltpu.get_barrier_semaphore()
    for m in range(1, 4):
        pl.semaphore_signal(barrier, 1, device_id=plane_peer(m, 0), device_id_type=MESH)
        pl.semaphore_signal(barrier, 1, device_id=plane_peer(0, m), device_id_type=MESH)
        pl.semaphore_signal(barrier, 1, device_id=z_peer(NEAR[m - 1]), device_id_type=MESH)

    def tokens(turn):
        for m in range(3):
            pl.semaphore_signal(token_sem.at[turn, m], 1, device_id=z_peer(NEAR[m]), device_id_type=MESH)

    def await_tokens(turn):
        for m in range(3):
            pl.semaphore_wait(token_sem.at[turn, m], 1)

    for step in range(STEPS):
        for table in range(2):
            load(step, table).start()
    challenge_copy = pltpu.make_async_copy(challenges_in, challenges, challenge_sem)
    challenge_copy.start()

    def raw_value(step, table, tile):
        low, middle, high = (raw[step, table, limb, tile].astype(I32) for limb in range(3))
        return low + lax.shift_left(middle, jnp.full(low.shape, 11, I32)) + lax.shift_left(high, jnp.full(low.shape, 22, I32))

    def prepare(step):
        for table in range(2):
            load(step, table).wait()

        def body(i, carry):
            k, t = i // TILES, i % TILES
            tile = (y + k + 1) % 4 * TILES + t
            for table in range(2):
                y_send[step, k, table, t] = encode(raw_value(step, table, tile))
            return carry

        lax.fori_loop(0, 3 * TILES, body, 0)

        def mine(t, carry):
            for table in range(2):
                own[step, table, t] = encode(raw_value(step, table, y * TILES + t))
            return carry

        lax.fori_loop(0, TILES, mine, 0)

    def send(step):
        for k in range(3):
            y_copy(step, k).start()

    def ahead(step, carry):
        prepare(step)
        send(step)
        return carry

    def prepare_early(e, outer):
        step = LATE + e
        for table in range(2):
            load(step, table).wait()

        def body(i, carry):
            k, quarter, t = i // TILES, i % TILES // PART, i % PART
            tile = quarter * TILES + (x + k + 1) % 4 * PART + t
            for table in range(2):
                early_send[e, k, table, quarter, t] = encode(raw_value(step, table, tile))
            return carry

        lax.fori_loop(0, 3 * TILES, body, 0)
        for k in range(3):
            early_copy(e, k).start()

        def mine(i, carry):
            k, t = i // PART, i % PART
            for table in range(2):
                y_send[step, k, table, 4 * t] = encode(raw_value(step, table, (y + k + 1) % 4 * TILES + x * PART + t))
            return carry

        lax.fori_loop(0, 3 * PART, mine, 0)
        for t in range(PART):
            for table in range(2):
                own[step, table, 4 * t] = encode(raw_value(step, table, y * TILES + x * PART + t))
        return outer

    def prepare_last(e, outer):
        step = LATE + e
        for k in range(3):
            early_copy(e, k).wait_recv()

        def body(i, carry):
            k, t = i // PART, i % PART
            for table in range(2):
                for d in range(3):
                    y_send[step, d, table, 4 * t + k + 1] = early_recv[e, k, table, (y + d + 1) % 4, t]
                own[step, table, 4 * t + k + 1] = early_recv[e, k, table, y, t]
            return carry

        lax.fori_loop(0, 3 * PART, body, 0)
        for t in range(PART):
            for k in range(3):
                last_copy(e, t, k).start()
        return outer

    prepare(0)
    pl.semaphore_wait(barrier, 9)
    send(0)
    tokens(0)
    lax.fori_loop(1, 2, ahead, 0)
    lax.fori_loop(0, EARLY, prepare_early, 0)
    lax.fori_loop(2, LATE, ahead, 0)
    await_tokens(0)
    tokens(1)
    lax.fori_loop(0, EARLY, prepare_last, 0)

    sums_ref[...] = jnp.zeros_like(sums_ref)

    def phase_scalars(position, first, second):
        behind = (position + 3) % 4
        return [
            scalar_parts(challenges[first], position // 2),
            scalar_parts(challenges[first], behind // 2),
            scalar_parts(challenges[second], position % 2),
        ]

    def load_sums(phase):
        return tuple((sums_ref[phase, i, 0], sums_ref[phase, i, 1]) for i in range(8))

    def store_sums(phase, sums):
        for i in range(8):
            for part in range(2):
                sums_ref[phase, i, part] = sums[i][part]

    challenge_copy.wait()
    y_scalars = phase_scalars(y, 0, 1)
    x_scalars = phase_scalars(x, 2, 3)

    def y_phase(step):
        for k in range(3):
            y_copy(step, k).wait_recv()

        def body(i, sums):
            part, t = i // PART, i % PART
            tile = (x + part) % 4 * PART + t
            tables = [
                [decode(own[step, table, tile])] + [decode(y_recv[step, k, table, tile]) for k in (1, 0, 2)]
                for table in range(2)
            ]
            select, proof, sums = two_rounds(tables[0], tables[1], sums, y_scalars)
            x_own[0, i], x_own[1, i] = select, proof
            return sums

        store_sums(0, lax.fori_loop(0, TILES, body, load_sums(0)))

        def coded(i, carry):
            k, t = i // PART, i % PART
            for table in range(2):
                x_send[step, k, table, t] = encode(x_own[table, PART + i])
            return carry

        lax.fori_loop(0, 3 * PART, coded, 0)

        for k in range(3):
            x_copy(step, k).start()
        for t in range(PART):
            for table in range(2):
                x_own[table, TILES + step * PART + t] = x_own[table, t]

    def finished(step, t, select, proof):
        for ref, value in ((out_selects, select), (out_proofs, proof)):
            ref[step, t] = jnp.where(value == MODULUS, 0, value)

    def x_phase(step):
        for k in range(3):
            x_copy(step, k).wait_recv()

        def body(t, sums):
            tables = [
                [x_own[table, TILES + step * PART + t]] + [decode(x_recv[step, k, table, t]) for k in (1, 0, 2)]
                for table in range(2)
            ]
            select, proof, sums = two_rounds(tables[0], tables[1], sums, x_scalars)
            finished(step, t, select, proof)
            return sums

        store_sums(1, lax.fori_loop(0, PART, body, load_sums(1)))

    def last_phase(e, t):
        step = LATE + e
        for k in range(3):
            last_copy(e, t, k).wait_recv()

        def body(r, sums):
            tables = [
                [decode(own[step, table, 4 * t + r])] + [decode(y_recv[step, k, table, 4 * t + r]) for k in (1, 0, 2)]
                for table in range(2)
            ]
            x_own[0, r], x_own[1, r], sums = two_rounds(tables[0], tables[1], sums, y_scalars)
            return sums

        store_sums(0, lax.fori_loop(0, 4, body, load_sums(0)))
        tables = [[x_own[table, r] for r in (0, 2, 1, 3)] for table in range(2)]
        select, proof, sums = two_rounds(tables[0], tables[1], load_sums(1), x_scalars)
        store_sums(1, sums)
        finished(step, t, select, proof)

    def main(step, carry):
        y_phase(step)

        @pl.when(step >= 1)
        def _():
            x_phase(step - 1)

        return carry

    lax.fori_loop(0, LATE, main, 0)

    def last(i, carry):
        last_phase(i // PART, i % PART)

        @pl.when(i == PART)
        def _():
            x_phase(LATE - 1)

        return carry

    lax.fori_loop(0, EARLY * PART, last, 0)

    row = lax.broadcasted_iota(I32, (8, 128), 0)
    lane = lax.broadcasted_iota(I32, (8, 128), 1)
    halves = [[jnp.zeros((8, 128), I32) for _ in range(2)] for _ in range(3)]
    for phase, position in ((0, y), (1, x)):
        own_high, behind_high, odd = position // 2, (position + 3) % 4 // 2, position % 2
        sums = load_sums(phase)
        points = []
        for part in range(2):
            own, ahead_two, behind, ahead_one, across, even_sum, odd_sum, across_next = (s[part] for s in sums)
            upper = own * own_high + ahead_two * (1 - own_high) + behind * behind_high + ahead_one * (1 - behind_high)
            lower = own + ahead_two + behind + ahead_one - upper
            second_upper = even_sum * odd + odd_sum * (1 - odd)
            second_lower = even_sum + odd_sum - second_upper
            points.append((lower, upper, across, second_lower, second_upper, across_next))
        for i in range(6):
            at_round, at_point = 2 * phase + i // 3, i % 3
            low, high = points[0][i], points[1][i]
            value = fold31(low + srl(high, 15) + lax.shift_left(high & 0x7FFF, jnp.full(high.shape, 16, I32)))
            for half, piece in enumerate(split(value)):
                for shift in (4, 2, 1):
                    piece = piece + pltpu.roll(piece, shift, 0)
                halves[at_point][half] += jnp.where(row == at_round, piece, 0)
    tile = jnp.zeros((8, 128), I32)
    for at_point in range(3):
        low, high = (across_tile(half) for half in halves[at_point])
        value = fold31(low + srl(high, 15))
        value = fold31(value + lax.shift_left(high & 0x7FFF, jnp.full(high.shape, 16, I32)))
        for limb, piece in enumerate((value & 2047, srl(value, 11) & 2047, srl(value, 22))):
            tile += jnp.where(lane == 3 * limb + at_point, piece, 0)
    tile_out[0] = tile.astype(F32)

    def plane_copy(m):
        return pltpu.make_async_remote_copy(
            tile_out.at[1, :4], gathered.at[m, :4], plane_send_sem.at[m], plane_recv_sem.at[m],
            device_id=plane_peer(m // 4, m % 4), device_id_type=MESH,
        )

    def z_copy(m):
        return pltpu.make_async_remote_copy(
            tile_out.at[0, :4], gathered_z.at[m, :4], z_send_sem.at[m], z_recv_sem.at[m],
            device_id=z_peer(m), device_id_type=MESH,
        )

    await_tokens(1)
    for m in range(1, 8):
        z_copy(m).start()

    def finish(step, carry):
        for k in range(3):
            y_copy(step, k).wait_send()
            x_copy(step, k).wait_send()
        return carry

    lax.fori_loop(0, LATE, finish, 0)

    def finish_last(e, carry):
        for k in range(3):
            early_copy(e, k).wait_send()
            for t in range(PART):
                last_copy(e, t, k).wait_send()
        return carry

    lax.fori_loop(0, EARLY, finish_last, 0)
    total = tile_out[0]
    for m in range(1, 8):
        z_copy(m).wait_recv()
        total = total + gathered_z[m]
    tile_out[1] = total
    for m in FAR_FIRST:
        plane_copy(m).start()
    for m in range(1, 8):
        z_copy(m).wait_send()
    for m in range(1, 16):
        plane_copy(m).wait_recv()
        total = total + gathered[m]

    limbs = total.astype(I32)
    middle, high = pltpu.roll(limbs, 125, 1), pltpu.roll(limbs, 122, 1)
    value = limbs + lax.shift_left(middle, jnp.full(middle.shape, 11, I32))
    value = fold31(value + srl(high, 9))
    value = fold31(value + lax.shift_left(high & 511, jnp.full(high.shape, 22, I32)))
    at_zero, at_one = pltpu.roll(value, 2, 1), pltpu.roll(value, 1, 1)
    at_two = fold31(fold31(value + value) + fold31(at_one + at_one))
    at_two = fold31(at_two + (MODULUS - at_zero))
    value = jnp.where(lane == 2, at_two, value)
    value = jnp.where(value == MODULUS, 0, value)
    for limb, piece in enumerate((value & 2047, srl(value, 11) & 2047, srl(value, 22))):
        out_points[limb] = piece.astype(F32)[:4, :3]

    for m in range(1, 16):
        plane_copy(m).wait_send()


def write(points, selects, proofs, out_points, out_selects, out_proofs):
    out_points[...] = points[...]
    for ints, out in ((selects, out_selects), (proofs, out_proofs)):
        v = ints[...]
        for limb, piece in enumerate((v & 2047, srl(v, 11) & 2047, srl(v, 22))):
            out[limb] = piece.astype(F32)


def shards(selectors, proofs, challenges):
    vmem = pl.BlockSpec(memory_space=pltpu.VMEM)
    tables = [t.reshape(3, 8, 64, 8, 128) for t in (selectors, proofs)]
    ints = pltpu.VMEM((STEPS, PART, 8, 128), I32)
    results = pl.pallas_call(
        kernel,
        out_shape=(pltpu.VMEM((3, 4, 3), F32), ints, ints),
        in_specs=[
            pl.BlockSpec(memory_space=pltpu.HBM),
            pl.BlockSpec(memory_space=pltpu.HBM),
            pl.BlockSpec(memory_space=pltpu.HBM),
        ],
        out_specs=(vmem, vmem, vmem),
        scratch_shapes=[
            pltpu.VMEM((STEPS, 2, 3, 64, 8, 128), F32),
            pltpu.VMEM((STEPS, 2, TILES, 8, 128), F32),
            pltpu.VMEM((STEPS, 3, 2, TILES, 8, 128), F32),
            pltpu.VMEM((STEPS, 3, 2, TILES, 8, 128), F32),
            pltpu.VMEM((EARLY, 3, 2, 4, PART, 8, 128), F32),
            pltpu.VMEM((EARLY, 3, 2, 4, PART, 8, 128), F32),
            pltpu.VMEM((2, TILES + STEPS * PART, 8, 128), I32),
            pltpu.VMEM((STEPS, 3, 2, PART, 8, 128), F32),
            pltpu.VMEM((STEPS, 3, 2, PART, 8, 128), F32),
            pltpu.VMEM((2, 8, 2, 8, 128), I32),
            pltpu.VMEM((16, 8, 128), F32),
            pltpu.VMEM((8, 8, 128), F32),
            pltpu.VMEM((2, 8, 128), F32),
            pltpu.SMEM((4,), I32),
            pltpu.SemaphoreType.DMA((STEPS, 2)),
            pltpu.SemaphoreType.DMA((STEPS, 3)),
            pltpu.SemaphoreType.DMA((STEPS, 3)),
            pltpu.SemaphoreType.DMA((EARLY, 3)),
            pltpu.SemaphoreType.DMA((EARLY, 3)),
            pltpu.SemaphoreType.DMA((STEPS, 3)),
            pltpu.SemaphoreType.DMA((STEPS, 3)),
            pltpu.SemaphoreType.DMA((EARLY, PART, 3)),
            pltpu.SemaphoreType.DMA((EARLY, PART, 3)),
            pltpu.SemaphoreType.DMA((16,)),
            pltpu.SemaphoreType.DMA((16,)),
            pltpu.SemaphoreType.DMA((8,)),
            pltpu.SemaphoreType.DMA((8,)),
            pltpu.SemaphoreType.REGULAR((2, 3)),
            pltpu.SemaphoreType.DMA,
        ],
        compiler_params=pltpu.CompilerParams(collective_id=0, has_side_effects=True, vmem_limit_bytes=40 << 20),
        name="sumcheck",
    )(*(pltpu.with_memory_space_constraint(t, pltpu.HBM) for t in (challenges, *tables)))
    limbs = jax.ShapeDtypeStruct((3, STEPS, PART, 8, 128), F32)
    points, selects, proofs_done = pl.pallas_call(
        write,
        out_shape=(jax.ShapeDtypeStruct((3, 4, 3), F32), limbs, limbs),
        in_specs=[vmem, vmem, vmem],
        out_specs=(vmem, vmem, vmem),
        name="write_limbs",
    )(*(pltpu.with_memory_space_constraint(r, pltpu.VMEM) for r in results))
    return points, selects.reshape(3, 8, 1, 1, 4096), proofs_done.reshape(3, 8, 1, 1, 4096)


def solution(mesh):
    tables = P(None, None, "gx", "gy", None)
    return jax.shard_map(shards, mesh=mesh, in_specs=(tables, tables, P()), out_specs=(P(), tables, tables), check_vma=False)
```

```python
import jax
import jax.numpy as jnp
from jax import lax
from jax.experimental import pallas as pl
from jax.experimental.pallas import tpu as pltpu
from jax.sharding import PartitionSpec as P

MESH = pl.DeviceIdType.MESH
I32 = jnp.int32
F32 = jnp.float32
MODULUS = 0x7FFFFFFF
STEPS = 8
EARLY = 2
LATE = STEPS - EARLY
TILES = 16
PART = 4
FAR_FIRST = (10, 9, 11, 6, 14, 5, 7, 13, 15, 2, 8, 1, 3, 4, 12)
NEAR = (1, 3, 4)


def srl(x, n):
    return lax.shift_right_logical(x, jnp.full(x.shape, n, I32))


def fold31(x):
    return (x & MODULUS) + srl(x, 31)


def encode(v):
    scaled = lax.shift_left((v & 0x7FFFFF) | 0x800000, srl(v, 23) & 7)
    power = lax.shift_left(jnp.full(v.shape, 1, I32), srl(v, 26) & 15).astype(F32)
    power = power * power
    power = power * power
    power = power * power
    unit = jnp.where(v >= 1 << 30, F32(-(2.0**-60)), F32(2.0**-60))
    return scaled.astype(F32) * unit * power


def decode(x):
    negative = x < 0
    a = jnp.abs(x)
    high = a >= F32(2.0**27)
    v = jnp.where(high, I32((1 << 29) - (1 << 23)), I32(-(1 << 23)))
    a = a * jnp.where(high, F32(2.0**-4), F32(2.0**60))
    for bit, shift in ((28, 32), (27, 16), (26, 8)):
        high = a >= F32(2.0 ** (23 + shift))
        v = v + jnp.where(high, I32(1 << bit), I32(0))
        a = a * jnp.where(high, F32(2.0**-shift), F32(1.0))
    v = v + jnp.where(negative, I32(1 << 30), I32(0))
    scaled = a.astype(I32)
    low = 8 - lax.clz(scaled)
    return v + lax.shift_right_logical(scaled, low) + lax.shift_left(low, jnp.full(low.shape, 23, I32))


def split(v):
    return v & 0xFFFF, srl(v, 16)


def difference(a, b):
    d = a - b
    return jnp.where(d < 0, d + MODULUS, d)


def add_product(sums, a, b):
    low = a[0] * b[0]
    middle = a[0] * b[1] + a[1] * b[0]
    high = (a[1] + a[1]) * b[1]
    return (
        sums[0] + ((low & 0xFFFF) + srl(middle, 15) + (high & 0xFFFF)),
        sums[1] + (srl(low, 16) + (middle & 0x7FFF) + srl(high, 16)),
    )


def folded(base, d, scalar):
    low = d[0] * scalar[0]
    middle = d[0] * scalar[1] + d[1] * scalar[0]
    t = fold31(low) + srl(middle, 15)
    t = fold31(t + d[1] * scalar[2])
    t = fold31(t + lax.shift_left(middle & 0x7FFF, jnp.full(middle.shape, 16, I32)))
    return fold31(t + base)


def two_rounds(selects, proofs, sums, scalars):
    select_parts, proof_parts = [split(v) for v in selects], [split(v) for v in proofs]
    sums = list(sums)
    for i in range(4):
        sums[i] = add_product(sums[i], select_parts[i], proof_parts[i])
    select_next, proof_next = [], []
    for pair in range(2):
        ds = split(difference(selects[2 * pair + 1], selects[2 * pair]))
        dp = split(difference(proofs[2 * pair + 1], proofs[2 * pair]))
        sums[4] = add_product(sums[4], ds, dp)
        select_next.append(folded(selects[2 * pair], ds, scalars[pair]))
        proof_next.append(folded(proofs[2 * pair], dp, scalars[pair]))
    for i in range(2):
        sums[5 + i] = add_product(sums[5 + i], split(select_next[i]), split(proof_next[i]))
    ds = split(difference(select_next[1], select_next[0]))
    dp = split(difference(proof_next[1], proof_next[0]))
    sums[7] = add_product(sums[7], ds, dp)
    return folded(select_next[0], ds, scalars[2]), folded(proof_next[0], dp, scalars[2]), tuple(sums)


def scalar_parts(challenge, flipped):
    other = 1 - challenge
    other = other + (lax.shift_right_arithmetic(other, I32(31)) & MODULUS)
    value = challenge * (1 - flipped) + other * flipped
    low, high = value & 0xFFFF, lax.shift_right_logical(value, I32(16))
    return [jnp.full((8, 128), s, I32) for s in (low, high, high + high)]


def across_tile(x):
    for shift in (64, 32, 16, 8, 4, 2, 1):
        x = x + pltpu.roll(x, shift, 1)
    return x


def kernel(
    challenges_in, selectors, proofs, out_points, out_selects, out_proofs,
    raw, own, y_send, y_recv, early_send, early_recv, x_own, x_send, x_recv, sums_ref, gathered, gathered_z, tile_out, challenges,
    raw_sem, y_send_sem, y_recv_sem, early_send_sem, early_recv_sem, x_send_sem, x_recv_sem,
    last_send_sem, last_recv_sem, plane_send_sem, plane_recv_sem, z_send_sem, z_recv_sem, token_sem, challenge_sem,
):
    gx, gy = lax.axis_index("gx"), lax.axis_index("gy")
    y, z_low = gx // 2, gx % 2
    x, z_core = gy // 4, gy % 4

    def plane_peer(dy, dx):
        return {"gx": (y + dy) % 4 * 2 + z_low, "gy": (x + dx) % 4 * 4 + z_core}

    def z_peer(m):
        z_high, core = z_core // 2, z_core % 2
        return {
            "gx": y * 2 + (z_low + m % 2) % 2,
            "gy": x * 4 + (z_high + m // 2 % 2) % 2 * 2 + (core + m // 4) % 2,
        }

    def load(step, table):
        source = (selectors, proofs)[table]
        return pltpu.make_async_copy(source.at[:, step], raw.at[step, table], raw_sem.at[step, table])

    def y_copy(step, k):
        return pltpu.make_async_remote_copy(
            y_send.at[step, k], y_recv.at[step, k], y_send_sem.at[step, k], y_recv_sem.at[step, k],
            device_id=plane_peer(k + 1, 0), device_id_type=MESH,
        )

    def last_copy(e, t, k):
        return pltpu.make_async_remote_copy(
            y_send.at[LATE + e, k, :, pl.ds(4 * t, 4)], y_recv.at[LATE + e, k, :, pl.ds(4 * t, 4)],
            last_send_sem.at[e, t, k], last_recv_sem.at[e, t, k],
            device_id=plane_peer(k + 1, 0), device_id_type=MESH,
        )

    def x_copy(step, k):
        return pltpu.make_async_remote_copy(
            x_send.at[step, k], x_recv.at[step, k], x_send_sem.at[step, k], x_recv_sem.at[step, k],
            device_id=plane_peer(0, k + 1), device_id_type=MESH,
        )

    def early_copy(e, k):
        return pltpu.make_async_remote_copy(
            early_send.at[e, k], early_recv.at[e, k], early_send_sem.at[e, k], early_recv_sem.at[e, k],
            device_id=plane_peer(0, k + 1), device_id_type=MESH,
        )

    gathered[...] = jnp.zeros_like(gathered)
    gathered_z[...] = jnp.zeros_like(gathered_z)

    barrier = pltpu.get_barrier_semaphore()
    for m in range(1, 4):
        pl.semaphore_signal(barrier, 1, device_id=plane_peer(m, 0), device_id_type=MESH)
        pl.semaphore_signal(barrier, 1, device_id=plane_peer(0, m), device_id_type=MESH)
        pl.semaphore_signal(barrier, 1, device_id=z_peer(NEAR[m - 1]), device_id_type=MESH)

    def tokens(turn):
        for m in range(3):
            pl.semaphore_signal(token_sem.at[turn, m], 1, device_id=z_peer(NEAR[m]), device_id_type=MESH)

    def await_tokens(turn):
        for m in range(3):
            pl.semaphore_wait(token_sem.at[turn, m], 1)

    for step in (0, 1, *range(LATE, STEPS), *range(2, LATE)):
        for table in range(2):
            load(step, table).start()
    challenge_copy = pltpu.make_async_copy(challenges_in, challenges, challenge_sem)
    challenge_copy.start()

    def raw_value(step, table, tile):
        low, middle, high = (raw[step, table, limb, tile].astype(I32) for limb in range(3))
        return low + lax.shift_left(middle, jnp.full(low.shape, 11, I32)) + lax.shift_left(high, jnp.full(low.shape, 22, I32))

    def prepare(step):
        for table in range(2):
            load(step, table).wait()

        def body(i, carry):
            k, t = i // TILES, i % TILES
            tile = (y + k + 1) % 4 * TILES + t
            for table in range(2):
                y_send[step, k, table, t] = encode(raw_value(step, table, tile))
            return carry

        lax.fori_loop(0, 3 * TILES, body, 0)

        def mine(t, carry):
            for table in range(2):
                own[step, table, t] = encode(raw_value(step, table, y * TILES + t))
            return carry

        lax.fori_loop(0, TILES, mine, 0)

    def send(step):
        for k in range(3):
            y_copy(step, k).start()

    def ahead(step, carry):
        prepare(step)
        send(step)
        return carry

    def prepare_early(e, outer):
        step = LATE + e
        for table in range(2):
            load(step, table).wait()

        def body(i, carry):
            k, quarter, t = i // TILES, i % TILES // PART, i % PART
            tile = quarter * TILES + (x + k + 1) % 4 * PART + t
            for table in range(2):
                early_send[e, k, table, quarter, t] = encode(raw_value(step, table, tile))
            return carry

        lax.fori_loop(0, 3 * TILES, body, 0)
        for k in range(3):
            early_copy(e, k).start()

        def mine(i, carry):
            k, t = i // PART, i % PART
            for table in range(2):
                y_send[step, k, table, 4 * t] = encode(raw_value(step, table, (y + k + 1) % 4 * TILES + x * PART + t))
            return carry

        lax.fori_loop(0, 3 * PART, mine, 0)
        for t in range(PART):
            for table in range(2):
                own[step, table, 4 * t] = encode(raw_value(step, table, y * TILES + x * PART + t))
        return outer

    def prepare_last(e, outer):
        step = LATE + e
        for k in range(3):
            early_copy(e, k).wait_recv()

        def body(i, carry):
            k, t = i // PART, i % PART
            for table in range(2):
                for d in range(3):
                    y_send[step, d, table, 4 * t + k + 1] = early_recv[e, k, table, (y + d + 1) % 4, t]
                own[step, table, 4 * t + k + 1] = early_recv[e, k, table, y, t]
            return carry

        lax.fori_loop(0, 3 * PART, body, 0)
        for t in range(PART):
            for k in range(3):
                last_copy(e, t, k).start()
        return outer

    prepare(0)
    pl.semaphore_wait(barrier, 9)
    send(0)
    tokens(0)
    lax.fori_loop(1, 2, ahead, 0)
    lax.fori_loop(0, EARLY, prepare_early, 0)
    lax.fori_loop(2, LATE, ahead, 0)
    await_tokens(0)
    tokens(1)
    lax.fori_loop(0, EARLY, prepare_last, 0)

    sums_ref[...] = jnp.zeros_like(sums_ref)

    def phase_scalars(position, first, second):
        behind = (position + 3) % 4
        return [
            scalar_parts(challenges[first], position // 2),
            scalar_parts(challenges[first], behind // 2),
            scalar_parts(challenges[second], position % 2),
        ]

    def load_sums(phase):
        return tuple((sums_ref[phase, i, 0], sums_ref[phase, i, 1]) for i in range(8))

    def store_sums(phase, sums):
        for i in range(8):
            for part in range(2):
                sums_ref[phase, i, part] = sums[i][part]

    challenge_copy.wait()
    y_scalars = phase_scalars(y, 0, 1)
    x_scalars = phase_scalars(x, 2, 3)

    def y_phase(step):
        for k in range(3):
            y_copy(step, k).wait_recv()

        def body(i, sums):
            part, t = i // PART, i % PART
            tile = (x + part) % 4 * PART + t
            tables = [
                [decode(own[step, table, tile])] + [decode(y_recv[step, k, table, tile]) for k in (1, 0, 2)]
                for table in range(2)
            ]
            select, proof, sums = two_rounds(tables[0], tables[1], sums, y_scalars)
            x_own[0, i], x_own[1, i] = select, proof
            return sums

        store_sums(0, lax.fori_loop(0, TILES, body, load_sums(0)))

        def coded(i, carry):
            k, t = i // PART, i % PART
            for table in range(2):
                x_send[step, k, table, t] = encode(x_own[table, PART + i])
            return carry

        lax.fori_loop(0, 3 * PART, coded, 0)

        for k in range(3):
            x_copy(step, k).start()
        for t in range(PART):
            for table in range(2):
                x_own[table, TILES + step * PART + t] = x_own[table, t]

    def finished(step, t, select, proof):
        for ref, value in ((out_selects, select), (out_proofs, proof)):
            ref[step, t] = jnp.where(value == MODULUS, 0, value)

    def x_phase(step):
        for k in range(3):
            x_copy(step, k).wait_recv()

        def body(t, sums):
            tables = [
                [x_own[table, TILES + step * PART + t]] + [decode(x_recv[step, k, table, t]) for k in (1, 0, 2)]
                for table in range(2)
            ]
            select, proof, sums = two_rounds(tables[0], tables[1], sums, x_scalars)
            finished(step, t, select, proof)
            return sums

        store_sums(1, lax.fori_loop(0, PART, body, load_sums(1)))

    def last_phase(e, t):
        step = LATE + e
        for k in range(3):
            last_copy(e, t, k).wait_recv()

        def body(r, sums):
            tables = [
                [decode(own[step, table, 4 * t + r])] + [decode(y_recv[step, k, table, 4 * t + r]) for k in (1, 0, 2)]
                for table in range(2)
            ]
            x_own[0, r], x_own[1, r], sums = two_rounds(tables[0], tables[1], sums, y_scalars)
            return sums

        sums = load_sums(0)
        for r in range(4):
            sums = body(r, sums)
        store_sums(0, sums)
        tables = [[x_own[table, r] for r in (0, 2, 1, 3)] for table in range(2)]
        select, proof, sums = two_rounds(tables[0], tables[1], load_sums(1), x_scalars)
        store_sums(1, sums)
        finished(step, t, select, proof)

    def main(step, carry):
        y_phase(step)

        @pl.when(step >= 1)
        def _():
            x_phase(step - 1)

        return carry

    lax.fori_loop(0, LATE, main, 0)

    def last(i, carry):
        last_phase(i // PART, i % PART)

        @pl.when(i == PART)
        def _():
            x_phase(LATE - 1)

        return carry

    lax.fori_loop(0, EARLY * PART, last, 0)

    row = lax.broadcasted_iota(I32, (8, 128), 0)
    lane = lax.broadcasted_iota(I32, (8, 128), 1)
    halves = [[jnp.zeros((8, 128), I32) for _ in range(2)] for _ in range(3)]
    for phase, position in ((0, y), (1, x)):
        own_high, behind_high, odd = position // 2, (position + 3) % 4 // 2, position % 2
        sums = load_sums(phase)
        points = []
        for part in range(2):
            own, ahead_two, behind, ahead_one, across, even_sum, odd_sum, across_next = (s[part] for s in sums)
            upper = own * own_high + ahead_two * (1 - own_high) + behind * behind_high + ahead_one * (1 - behind_high)
            lower = own + ahead_two + behind + ahead_one - upper
            second_upper = even_sum * odd + odd_sum * (1 - odd)
            second_lower = even_sum + odd_sum - second_upper
            points.append((lower, upper, across, second_lower, second_upper, across_next))
        for i in range(6):
            at_round, at_point = 2 * phase + i // 3, i % 3
            low, high = points[0][i], points[1][i]
            value = fold31(low + srl(high, 15) + lax.shift_left(high & 0x7FFF, jnp.full(high.shape, 16, I32)))
            for half, piece in enumerate(split(value)):
                for shift in (4, 2, 1):
                    piece = piece + pltpu.roll(piece, shift, 0)
                halves[at_point][half] += jnp.where(row == at_round, piece, 0)
    tile = jnp.zeros((8, 128), I32)
    for at_point in range(3):
        low, high = (across_tile(half) for half in halves[at_point])
        value = fold31(low + srl(high, 15))
        value = fold31(value + lax.shift_left(high & 0x7FFF, jnp.full(high.shape, 16, I32)))
        for limb, piece in enumerate((value & 2047, srl(value, 11) & 2047, srl(value, 22))):
            tile += jnp.where(lane == 3 * limb + at_point, piece, 0)
    tile_out[0] = tile.astype(F32)

    def plane_copy(m):
        return pltpu.make_async_remote_copy(
            tile_out.at[1, :4], gathered.at[m, :4], plane_send_sem.at[m], plane_recv_sem.at[m],
            device_id=plane_peer(m // 4, m % 4), device_id_type=MESH,
        )

    def z_copy(m):
        return pltpu.make_async_remote_copy(
            tile_out.at[0, :4], gathered_z.at[m, :4], z_send_sem.at[m], z_recv_sem.at[m],
            device_id=z_peer(m), device_id_type=MESH,
        )

    await_tokens(1)
    for m in range(1, 8):
        z_copy(m).start()

    def finish(step, carry):
        for k in range(3):
            y_copy(step, k).wait_send()
            x_copy(step, k).wait_send()
        return carry

    lax.fori_loop(0, LATE, finish, 0)

    def finish_last(e, carry):
        for k in range(3):
            early_copy(e, k).wait_send()
            for t in range(PART):
                last_copy(e, t, k).wait_send()
        return carry

    lax.fori_loop(0, EARLY, finish_last, 0)
    total = tile_out[0]
    for m in range(1, 8):
        z_copy(m).wait_recv()
        total = total + gathered_z[m]
    tile_out[1] = total
    for m in FAR_FIRST:
        plane_copy(m).start()
    for m in range(1, 8):
        z_copy(m).wait_send()
    for m in range(1, 16):
        plane_copy(m).wait_recv()
        total = total + gathered[m]

    limbs = total.astype(I32)
    middle, high = pltpu.roll(limbs, 125, 1), pltpu.roll(limbs, 122, 1)
    value = limbs + lax.shift_left(middle, jnp.full(middle.shape, 11, I32))
    value = fold31(value + srl(high, 9))
    value = fold31(value + lax.shift_left(high & 511, jnp.full(high.shape, 22, I32)))
    at_zero, at_one = pltpu.roll(value, 2, 1), pltpu.roll(value, 1, 1)
    at_two = fold31(fold31(value + value) + fold31(at_one + at_one))
    at_two = fold31(at_two + (MODULUS - at_zero))
    value = jnp.where(lane == 2, at_two, value)
    value = jnp.where(value == MODULUS, 0, value)
    for limb, piece in enumerate((value & 2047, srl(value, 11) & 2047, srl(value, 22))):
        out_points[limb] = piece.astype(F32)[:4, :3]

    for m in range(1, 16):
        plane_copy(m).wait_send()


def write(points, selects, proofs, out_points, out_selects, out_proofs):
    out_points[...] = points[...]
    for ints, out in ((selects, out_selects), (proofs, out_proofs)):
        v = ints[...]
        for limb, piece in enumerate((v & 2047, srl(v, 11) & 2047, srl(v, 22))):
            out[limb] = piece.astype(F32)


def shards(selectors, proofs, challenges):
    vmem = pl.BlockSpec(memory_space=pltpu.VMEM)
    tables = [t.reshape(3, 8, 64, 8, 128) for t in (selectors, proofs)]
    ints = pltpu.VMEM((STEPS, PART, 8, 128), I32)
    results = pl.pallas_call(
        kernel,
        out_shape=(pltpu.VMEM((3, 4, 3), F32), ints, ints),
        in_specs=[
            pl.BlockSpec(memory_space=pltpu.HBM),
            pl.BlockSpec(memory_space=pltpu.HBM),
            pl.BlockSpec(memory_space=pltpu.HBM),
        ],
        out_specs=(vmem, vmem, vmem),
        scratch_shapes=[
            pltpu.VMEM((STEPS, 2, 3, 64, 8, 128), F32),
            pltpu.VMEM((STEPS, 2, TILES, 8, 128), F32),
            pltpu.VMEM((STEPS, 3, 2, TILES, 8, 128), F32),
            pltpu.VMEM((STEPS, 3, 2, TILES, 8, 128), F32),
            pltpu.VMEM((EARLY, 3, 2, 4, PART, 8, 128), F32),
            pltpu.VMEM((EARLY, 3, 2, 4, PART, 8, 128), F32),
            pltpu.VMEM((2, TILES + STEPS * PART, 8, 128), I32),
            pltpu.VMEM((STEPS, 3, 2, PART, 8, 128), F32),
            pltpu.VMEM((STEPS, 3, 2, PART, 8, 128), F32),
            pltpu.VMEM((2, 8, 2, 8, 128), I32),
            pltpu.VMEM((16, 8, 128), F32),
            pltpu.VMEM((8, 8, 128), F32),
            pltpu.VMEM((2, 8, 128), F32),
            pltpu.SMEM((4,), I32),
            pltpu.SemaphoreType.DMA((STEPS, 2)),
            pltpu.SemaphoreType.DMA((STEPS, 3)),
            pltpu.SemaphoreType.DMA((STEPS, 3)),
            pltpu.SemaphoreType.DMA((EARLY, 3)),
            pltpu.SemaphoreType.DMA((EARLY, 3)),
            pltpu.SemaphoreType.DMA((STEPS, 3)),
            pltpu.SemaphoreType.DMA((STEPS, 3)),
            pltpu.SemaphoreType.DMA((EARLY, PART, 3)),
            pltpu.SemaphoreType.DMA((EARLY, PART, 3)),
            pltpu.SemaphoreType.DMA((16,)),
            pltpu.SemaphoreType.DMA((16,)),
            pltpu.SemaphoreType.DMA((8,)),
            pltpu.SemaphoreType.DMA((8,)),
            pltpu.SemaphoreType.REGULAR((2, 3)),
            pltpu.SemaphoreType.DMA,
        ],
        compiler_params=pltpu.CompilerParams(collective_id=0, has_side_effects=True, vmem_limit_bytes=40 << 20),
        name="sumcheck",
    )(*(pltpu.with_memory_space_constraint(t, pltpu.HBM) for t in (challenges, *tables)))
    limbs = jax.ShapeDtypeStruct((3, STEPS, PART, 8, 128), F32)
    points, selects, proofs_done = pl.pallas_call(
        write,
        out_shape=(jax.ShapeDtypeStruct((3, 4, 3), F32), limbs, limbs),
        in_specs=[vmem, vmem, vmem],
        out_specs=(vmem, vmem, vmem),
        name="write_limbs",
    )(*(pltpu.with_memory_space_constraint(r, pltpu.VMEM) for r in results))
    return points, selects.reshape(3, 8, 1, 1, 4096), proofs_done.reshape(3, 8, 1, 1, 4096)


def solution(mesh):
    tables = P(None, None, "gx", "gy", None)
    return jax.shard_map(shards, mesh=mesh, in_specs=(tables, tables, P()), out_specs=(P(), tables, tables), check_vma=False)
```

```python
import jax
import jax.numpy as jnp
from jax import lax
from jax.experimental import pallas as pl
from jax.experimental.pallas import tpu as pltpu
from jax.sharding import PartitionSpec as P

MESH = pl.DeviceIdType.MESH
I32 = jnp.int32
F32 = jnp.float32
MODULUS = 0x7FFFFFFF
STEPS = 8
EARLY = 2
LATE = STEPS - EARLY
TILES = 16
PART = 4
FAR_FIRST = (10, 9, 11, 6, 14, 5, 7, 13, 15, 2, 8, 1, 3, 4, 12)
NEAR = (1, 3, 4)


def srl(x, n):
    return lax.shift_right_logical(x, jnp.full(x.shape, n, I32))


def fold31(x):
    return (x & MODULUS) + srl(x, 31)


def encode(v):
    scaled = lax.shift_left((v & 0x7FFFFF) | 0x800000, srl(v, 23) & 7)
    power = lax.shift_left(jnp.full(v.shape, 1, I32), srl(v, 26) & 15).astype(F32)
    power = power * power
    power = power * power
    power = power * power
    unit = jnp.where(v >= 1 << 30, F32(-(2.0**-60)), F32(2.0**-60))
    return scaled.astype(F32) * unit * power


def decode(x):
    negative = x < 0
    a = jnp.abs(x)
    high = a >= F32(2.0**27)
    v = jnp.where(high, I32((1 << 29) - (1 << 23)), I32(-(1 << 23)))
    a = a * jnp.where(high, F32(2.0**-4), F32(2.0**60))
    for bit, shift in ((28, 32), (27, 16), (26, 8)):
        high = a >= F32(2.0 ** (23 + shift))
        v = v + jnp.where(high, I32(1 << bit), I32(0))
        a = a * jnp.where(high, F32(2.0**-shift), F32(1.0))
    v = v + jnp.where(negative, I32(1 << 30), I32(0))
    scaled = a.astype(I32)
    low = 8 - lax.clz(scaled)
    return v + lax.shift_right_logical(scaled, low) + lax.shift_left(low, jnp.full(low.shape, 23, I32))


def split(v):
    return v & 0xFFFF, srl(v, 16)


def difference(a, b):
    d = a - b
    return jnp.where(d < 0, d + MODULUS, d)


def add_product(sums, a, b):
    low = a[0] * b[0]
    middle = a[0] * b[1] + a[1] * b[0]
    high = (a[1] + a[1]) * b[1]
    return (
        sums[0] + ((low & 0xFFFF) + srl(middle, 15) + (high & 0xFFFF)),
        sums[1] + (srl(low, 16) + (middle & 0x7FFF) + srl(high, 16)),
    )


def folded(base, d, scalar):
    low = d[0] * scalar[0]
    middle = d[0] * scalar[1] + d[1] * scalar[0]
    t = fold31(low) + srl(middle, 15)
    t = fold31(t + d[1] * scalar[2])
    t = fold31(t + lax.shift_left(middle & 0x7FFF, jnp.full(middle.shape, 16, I32)))
    return fold31(t + base)


def two_rounds(selects, proofs, sums, scalars):
    select_parts, proof_parts = [split(v) for v in selects], [split(v) for v in proofs]
    sums = list(sums)
    for i in range(4):
        sums[i] = add_product(sums[i], select_parts[i], proof_parts[i])
    select_next, proof_next = [], []
    for pair in range(2):
        ds = split(difference(selects[2 * pair + 1], selects[2 * pair]))
        dp = split(difference(proofs[2 * pair + 1], proofs[2 * pair]))
        sums[4] = add_product(sums[4], ds, dp)
        select_next.append(folded(selects[2 * pair], ds, scalars[pair]))
        proof_next.append(folded(proofs[2 * pair], dp, scalars[pair]))
    for i in range(2):
        sums[5 + i] = add_product(sums[5 + i], split(select_next[i]), split(proof_next[i]))
    ds = split(difference(select_next[1], select_next[0]))
    dp = split(difference(proof_next[1], proof_next[0]))
    sums[7] = add_product(sums[7], ds, dp)
    return folded(select_next[0], ds, scalars[2]), folded(proof_next[0], dp, scalars[2]), tuple(sums)


def scalar_parts(challenge, flipped):
    other = 1 - challenge
    other = other + (lax.shift_right_arithmetic(other, I32(31)) & MODULUS)
    value = challenge * (1 - flipped) + other * flipped
    low, high = value & 0xFFFF, lax.shift_right_logical(value, I32(16))
    return [jnp.full((8, 128), s, I32) for s in (low, high, high + high)]


def across_tile(x):
    for shift in (64, 32, 16, 8, 4, 2, 1):
        x = x + pltpu.roll(x, shift, 1)
    return x


def kernel(
    challenges_in, selectors, proofs, out_points, out_selects, out_proofs,
    raw, own, y_send, y_recv, early_send, early_recv, x_own, x_send, x_recv, sums_ref, gathered, gathered_z, tile_out, challenges,
    raw_sem, y_send_sem, y_recv_sem, early_send_sem, early_recv_sem, x_send_sem, x_recv_sem,
    last_send_sem, last_recv_sem, plane_send_sem, plane_recv_sem, z_send_sem, z_recv_sem, token_sem, challenge_sem,
):
    gx, gy = lax.axis_index("gx"), lax.axis_index("gy")
    y, z_low = gx // 2, gx % 2
    x, z_core = gy // 4, gy % 4

    def plane_peer(dy, dx):
        return {"gx": lax.rem(y + dy, 4) * 2 + z_low, "gy": lax.rem(x + dx, 4) * 4 + z_core}

    def z_peer(m):
        z_high, core = z_core // 2, z_core % 2
        return {
            "gx": y * 2 + lax.rem(z_low + m % 2, 2),
            "gy": x * 4 + lax.rem(z_high + m // 2 % 2, 2) * 2 + lax.rem(core + m // 4, 2),
        }

    def load(step, table):
        source = (selectors, proofs)[table]
        return pltpu.make_async_copy(source.at[:, step], raw.at[step, table], raw_sem.at[step, table])

    def y_copy(step, k):
        return pltpu.make_async_remote_copy(
            y_send.at[step, k], y_recv.at[step, k], y_send_sem.at[step, k], y_recv_sem.at[step, k],
            device_id=plane_peer(k + 1, 0), device_id_type=MESH,
        )

    def last_copy(e, t, k):
        return pltpu.make_async_remote_copy(
            y_send.at[LATE + e, k, :, pl.ds(4 * t, 4)], y_recv.at[LATE + e, k, :, pl.ds(4 * t, 4)],
            last_send_sem.at[e, t, k], last_recv_sem.at[e, t, k],
            device_id=plane_peer(k + 1, 0), device_id_type=MESH,
        )

    def x_copy(step, k):
        return pltpu.make_async_remote_copy(
            x_send.at[step, k], x_recv.at[step, k], x_send_sem.at[step, k], x_recv_sem.at[step, k],
            device_id=plane_peer(0, k + 1), device_id_type=MESH,
        )

    def early_copy(e, k):
        return pltpu.make_async_remote_copy(
            early_send.at[e, k], early_recv.at[e, k], early_send_sem.at[e, k], early_recv_sem.at[e, k],
            device_id=plane_peer(0, k + 1), device_id_type=MESH,
        )

    gathered[...] = jnp.zeros_like(gathered)
    gathered_z[...] = jnp.zeros_like(gathered_z)

    barrier = pltpu.get_barrier_semaphore()
    for m in range(1, 4):
        pl.semaphore_signal(barrier, 1, device_id=plane_peer(m, 0), device_id_type=MESH)
        pl.semaphore_signal(barrier, 1, device_id=plane_peer(0, m), device_id_type=MESH)
        pl.semaphore_signal(barrier, 1, device_id=z_peer(NEAR[m - 1]), device_id_type=MESH)

    def tokens(turn):
        for m in range(3):
            pl.semaphore_signal(token_sem.at[turn, m], 1, device_id=z_peer(NEAR[m]), device_id_type=MESH)

    def await_tokens(turn):
        for m in range(3):
            pl.semaphore_wait(token_sem.at[turn, m], 1)

    for step in (0, 1, *range(LATE, STEPS), *range(2, LATE)):
        for table in range(2):
            load(step, table).start()
    challenge_copy = pltpu.make_async_copy(challenges_in, challenges, challenge_sem)
    challenge_copy.start()

    def raw_value(step, table, tile):
        low, middle, high = (raw[step, table, limb, tile].astype(I32) for limb in range(3))
        return low + lax.shift_left(middle, jnp.full(low.shape, 11, I32)) + lax.shift_left(high, jnp.full(low.shape, 22, I32))

    def prepare(step):
        for table in range(2):
            load(step, table).wait()

        def body(i, carry):
            k, t = lax.div(i, TILES), lax.rem(i, TILES)
            tile = lax.rem(y + k + 1, 4) * TILES + t
            for table in range(2):
                y_send[step, k, table, t] = encode(raw_value(step, table, tile))
            return carry

        lax.fori_loop(0, 3 * TILES, body, 0)

        def mine(t, carry):
            for table in range(2):
                own[step, table, t] = encode(raw_value(step, table, y * TILES + t))
            return carry

        lax.fori_loop(0, TILES, mine, 0)

    def send(step):
        for k in range(3):
            y_copy(step, k).start()

    def ahead(step, carry):
        prepare(step)
        send(step)
        return carry

    def prepare_early(e, outer):
        step = LATE + e
        for table in range(2):
            load(step, table).wait()

        def body(i, carry):
            k, quarter, t = i // TILES, i % TILES // PART, i % PART
            tile = quarter * TILES + (x + k + 1) % 4 * PART + t
            for table in range(2):
                early_send[e, k, table, quarter, t] = encode(raw_value(step, table, tile))
            return carry

        lax.fori_loop(0, 3 * TILES, body, 0)
        for k in range(3):
            early_copy(e, k).start()

        def mine(i, carry):
            k, t = lax.div(i, PART), lax.rem(i, PART)
            for table in range(2):
                y_send[step, k, table, 4 * t] = encode(raw_value(step, table, (y + k + 1) % 4 * TILES + x * PART + t))
            return carry

        lax.fori_loop(0, 3 * PART, mine, 0)
        for t in range(PART):
            for table in range(2):
                own[step, table, 4 * t] = encode(raw_value(step, table, y * TILES + x * PART + t))
        return outer

    def prepare_last(e, outer):
        step = LATE + e
        for k in range(3):
            early_copy(e, k).wait_recv()

        def body(i, carry):
            k, t = lax.div(i, PART), lax.rem(i, PART)
            for table in range(2):
                for d in range(3):
                    y_send[step, d, table, 4 * t + k + 1] = early_recv[e, k, table, (y + d + 1) % 4, t]
                own[step, table, 4 * t + k + 1] = early_recv[e, k, table, y, t]
            return carry

        lax.fori_loop(0, 3 * PART, body, 0)
        for t in range(PART):
            for k in range(3):
                last_copy(e, t, k).start()
        return outer

    prepare(0)
    pl.semaphore_wait(barrier, 9)
    send(0)
    tokens(0)
    lax.fori_loop(1, 2, ahead, 0)
    lax.fori_loop(0, EARLY, prepare_early, 0)
    lax.fori_loop(2, LATE, ahead, 0)
    await_tokens(0)
    tokens(1)
    lax.fori_loop(0, EARLY, prepare_last, 0)

    sums_ref[...] = jnp.zeros_like(sums_ref)

    def phase_scalars(position, first, second):
        behind = (position + 3) % 4
        return [
            scalar_parts(challenges[first], position // 2),
            scalar_parts(challenges[first], behind // 2),
            scalar_parts(challenges[second], position % 2),
        ]

    def load_sums(phase):
        return tuple((sums_ref[phase, i, 0], sums_ref[phase, i, 1]) for i in range(8))

    def store_sums(phase, sums):
        for i in range(8):
            for part in range(2):
                sums_ref[phase, i, part] = sums[i][part]

    challenge_copy.wait()
    y_scalars = phase_scalars(y, 0, 1)
    x_scalars = phase_scalars(x, 2, 3)

    def y_phase(step):
        for k in range(3):
            y_copy(step, k).wait_recv()

        def body(i, sums):
            part, t = lax.div(i, PART), lax.rem(i, PART)
            tile = lax.rem(x + part, 4) * PART + t
            tables = [
                [decode(own[step, table, tile])] + [decode(y_recv[step, k, table, tile]) for k in (1, 0, 2)]
                for table in range(2)
            ]
            select, proof, sums = two_rounds(tables[0], tables[1], sums, y_scalars)
            x_own[0, i], x_own[1, i] = select, proof
            return sums

        store_sums(0, lax.fori_loop(0, TILES, body, load_sums(0)))

        def coded(i, carry):
            k, t = lax.div(i, PART), lax.rem(i, PART)
            for table in range(2):
                x_send[step, k, table, t] = encode(x_own[table, PART + i])
            return carry

        lax.fori_loop(0, 3 * PART, coded, 0)

        for k in range(3):
            x_copy(step, k).start()
        for t in range(PART):
            for table in range(2):
                x_own[table, TILES + step * PART + t] = x_own[table, t]

    def finished(step, t, select, proof):
        for ref, value in ((out_selects, select), (out_proofs, proof)):
            ref[step, t] = jnp.where(value == MODULUS, 0, value)

    def x_phase(step):
        for k in range(3):
            x_copy(step, k).wait_recv()

        def body(t, sums):
            tables = [
                [x_own[table, TILES + step * PART + t]] + [decode(x_recv[step, k, table, t]) for k in (1, 0, 2)]
                for table in range(2)
            ]
            select, proof, sums = two_rounds(tables[0], tables[1], sums, x_scalars)
            finished(step, t, select, proof)
            return sums

        store_sums(1, lax.fori_loop(0, PART, body, load_sums(1)))

    def last_phase(e, t):
        step = LATE + e
        for k in range(3):
            last_copy(e, t, k).wait_recv()

        def body(r, sums):
            tables = [
                [decode(own[step, table, 4 * t + r])] + [decode(y_recv[step, k, table, 4 * t + r]) for k in (1, 0, 2)]
                for table in range(2)
            ]
            x_own[0, r], x_own[1, r], sums = two_rounds(tables[0], tables[1], sums, y_scalars)
            return sums

        sums = load_sums(0)
        for r in range(4):
            sums = body(r, sums)
        store_sums(0, sums)
        tables = [[x_own[table, r] for r in (0, 2, 1, 3)] for table in range(2)]
        select, proof, sums = two_rounds(tables[0], tables[1], load_sums(1), x_scalars)
        store_sums(1, sums)
        finished(step, t, select, proof)

    def main(step, carry):
        y_phase(step)

        @pl.when(step >= 1)
        def _():
            x_phase(step - 1)

        return carry

    lax.fori_loop(0, LATE, main, 0)

    def last(i, carry):
        last_phase(i // PART, i % PART)

        @pl.when(i == PART)
        def _():
            x_phase(LATE - 1)

        return carry

    lax.fori_loop(0, EARLY * PART, last, 0)

    row = lax.broadcasted_iota(I32, (8, 128), 0)
    lane = lax.broadcasted_iota(I32, (8, 128), 1)
    halves = [[jnp.zeros((8, 128), I32) for _ in range(2)] for _ in range(3)]
    for phase, position in ((0, y), (1, x)):
        own_high, behind_high, odd = position // 2, (position + 3) % 4 // 2, position % 2
        sums = load_sums(phase)
        points = []
        for part in range(2):
            own, ahead_two, behind, ahead_one, across, even_sum, odd_sum, across_next = (s[part] for s in sums)
            upper = own * own_high + ahead_two * (1 - own_high) + behind * behind_high + ahead_one * (1 - behind_high)
            lower = own + ahead_two + behind + ahead_one - upper
            second_upper = even_sum * odd + odd_sum * (1 - odd)
            second_lower = even_sum + odd_sum - second_upper
            points.append((lower, upper, across, second_lower, second_upper, across_next))
        for i in range(6):
            at_round, at_point = 2 * phase + i // 3, i % 3
            low, high = points[0][i], points[1][i]
            value = fold31(low + srl(high, 15) + lax.shift_left(high & 0x7FFF, jnp.full(high.shape, 16, I32)))
            for half, piece in enumerate(split(value)):
                for shift in (4, 2, 1):
                    piece = piece + pltpu.roll(piece, shift, 0)
                halves[at_point][half] += jnp.where(row == at_round, piece, 0)
    tile = jnp.zeros((8, 128), I32)
    for at_point in range(3):
        low, high = (across_tile(half) for half in halves[at_point])
        value = fold31(low + srl(high, 15))
        value = fold31(value + lax.shift_left(high & 0x7FFF, jnp.full(high.shape, 16, I32)))
        for limb, piece in enumerate((value & 2047, srl(value, 11) & 2047, srl(value, 22))):
            tile += jnp.where(lane == 3 * limb + at_point, piece, 0)
    tile_out[0] = tile.astype(F32)

    def plane_copy(m):
        return pltpu.make_async_remote_copy(
            tile_out.at[1, :4], gathered.at[m, :4], plane_send_sem.at[m], plane_recv_sem.at[m],
            device_id=plane_peer(m // 4, m % 4), device_id_type=MESH,
        )

    def z_copy(m):
        return pltpu.make_async_remote_copy(
            tile_out.at[0, :4], gathered_z.at[m, :4], z_send_sem.at[m], z_recv_sem.at[m],
            device_id=z_peer(m), device_id_type=MESH,
        )

    await_tokens(1)
    for m in range(1, 8):
        z_copy(m).start()

    def finish(step, carry):
        for k in range(3):
            y_copy(step, k).wait_send()
            x_copy(step, k).wait_send()
        return carry

    lax.fori_loop(0, LATE, finish, 0)

    def finish_last(e, carry):
        for k in range(3):
            early_copy(e, k).wait_send()
            for t in range(PART):
                last_copy(e, t, k).wait_send()
        return carry

    lax.fori_loop(0, EARLY, finish_last, 0)
    total = tile_out[0]
    for m in range(1, 8):
        z_copy(m).wait_recv()
        total = total + gathered_z[m]
    tile_out[1] = total
    for m in FAR_FIRST:
        plane_copy(m).start()
    for m in range(1, 8):
        z_copy(m).wait_send()
    for m in range(1, 16):
        plane_copy(m).wait_recv()
        total = total + gathered[m]

    limbs = total.astype(I32)
    middle, high = pltpu.roll(limbs, 125, 1), pltpu.roll(limbs, 122, 1)
    value = limbs + lax.shift_left(middle, jnp.full(middle.shape, 11, I32))
    value = fold31(value + srl(high, 9))
    value = fold31(value + lax.shift_left(high & 511, jnp.full(high.shape, 22, I32)))
    at_zero, at_one = pltpu.roll(value, 2, 1), pltpu.roll(value, 1, 1)
    at_two = fold31(fold31(value + value) + fold31(at_one + at_one))
    at_two = fold31(at_two + (MODULUS - at_zero))
    value = jnp.where(lane == 2, at_two, value)
    value = jnp.where(value == MODULUS, 0, value)
    for limb, piece in enumerate((value & 2047, srl(value, 11) & 2047, srl(value, 22))):
        out_points[limb] = piece.astype(F32)[:4, :3]

    for m in range(1, 16):
        plane_copy(m).wait_send()


def write(points, selects, proofs, out_points, out_selects, out_proofs):
    out_points[...] = points[...]
    for ints, out in ((selects, out_selects), (proofs, out_proofs)):
        v = ints[...]
        for limb, piece in enumerate((v & 2047, srl(v, 11) & 2047, srl(v, 22))):
            out[limb] = piece.astype(F32)


def shards(selectors, proofs, challenges):
    vmem = pl.BlockSpec(memory_space=pltpu.VMEM)
    tables = [t.reshape(3, 8, 64, 8, 128) for t in (selectors, proofs)]
    ints = pltpu.VMEM((STEPS, PART, 8, 128), I32)
    results = pl.pallas_call(
        kernel,
        out_shape=(pltpu.VMEM((3, 4, 3), F32), ints, ints),
        in_specs=[
            pl.BlockSpec(memory_space=pltpu.HBM),
            pl.BlockSpec(memory_space=pltpu.HBM),
            pl.BlockSpec(memory_space=pltpu.HBM),
        ],
        out_specs=(vmem, vmem, vmem),
        scratch_shapes=[
            pltpu.VMEM((STEPS, 2, 3, 64, 8, 128), F32),
            pltpu.VMEM((STEPS, 2, TILES, 8, 128), F32),
            pltpu.VMEM((STEPS, 3, 2, TILES, 8, 128), F32),
            pltpu.VMEM((STEPS, 3, 2, TILES, 8, 128), F32),
            pltpu.VMEM((EARLY, 3, 2, 4, PART, 8, 128), F32),
            pltpu.VMEM((EARLY, 3, 2, 4, PART, 8, 128), F32),
            pltpu.VMEM((2, TILES + STEPS * PART, 8, 128), I32),
            pltpu.VMEM((STEPS, 3, 2, PART, 8, 128), F32),
            pltpu.VMEM((STEPS, 3, 2, PART, 8, 128), F32),
            pltpu.VMEM((2, 8, 2, 8, 128), I32),
            pltpu.VMEM((16, 8, 128), F32),
            pltpu.VMEM((8, 8, 128), F32),
            pltpu.VMEM((2, 8, 128), F32),
            pltpu.SMEM((4,), I32),
            pltpu.SemaphoreType.DMA((STEPS, 2)),
            pltpu.SemaphoreType.DMA((STEPS, 3)),
            pltpu.SemaphoreType.DMA((STEPS, 3)),
            pltpu.SemaphoreType.DMA((EARLY, 3)),
            pltpu.SemaphoreType.DMA((EARLY, 3)),
            pltpu.SemaphoreType.DMA((STEPS, 3)),
            pltpu.SemaphoreType.DMA((STEPS, 3)),
            pltpu.SemaphoreType.DMA((EARLY, PART, 3)),
            pltpu.SemaphoreType.DMA((EARLY, PART, 3)),
            pltpu.SemaphoreType.DMA((16,)),
            pltpu.SemaphoreType.DMA((16,)),
            pltpu.SemaphoreType.DMA((8,)),
            pltpu.SemaphoreType.DMA((8,)),
            pltpu.SemaphoreType.REGULAR((2, 3)),
            pltpu.SemaphoreType.DMA,
        ],
        compiler_params=pltpu.CompilerParams(collective_id=0, has_side_effects=True, vmem_limit_bytes=40 << 20),
        name="sumcheck",
    )(*(pltpu.with_memory_space_constraint(t, pltpu.HBM) for t in (challenges, *tables)))
    limbs = jax.ShapeDtypeStruct((3, STEPS, PART, 8, 128), F32)
    points, selects, proofs_done = pl.pallas_call(
        write,
        out_shape=(jax.ShapeDtypeStruct((3, 4, 3), F32), limbs, limbs),
        in_specs=[vmem, vmem, vmem],
        out_specs=(vmem, vmem, vmem),
        name="write_limbs",
    )(*(pltpu.with_memory_space_constraint(r, pltpu.VMEM) for r in results))
    return points, selects.reshape(3, 8, 1, 1, 4096), proofs_done.reshape(3, 8, 1, 1, 4096)


def solution(mesh):
    tables = P(None, None, "gx", "gy", None)
    return jax.shard_map(shards, mesh=mesh, in_specs=(tables, tables, P()), out_specs=(P(), tables, tables), check_vma=False)
```
